32 devices in a mesh: rep: 4 (over z), slab: 8 (over y, x, core).
Axes of the slice: x: 2, y: 2, z: 4, core: 2. Of those that a mesh axis runs over, the one named last changes fastest.
Arguments:
- feats: bfloat16 [4, 32, 12288], P('rep', None, 'slab'), may hold values from -6 to 6
- tile_weight: bfloat16 [4, 768, 64, 512], P('rep', 'slab'), may hold values from -0.25 to 0.25
- tile_atom: int32 [4, 768], P('rep', 'slab'), may hold values from 0 to 23
- tile_cell: int32 [4, 768], P('rep', 'slab'), may hold values from 0 to 31
- tile_live: int32 [4, 8], P('rep', 'slab'), may hold values from 24 to 96, as said below
- w_mix: bfloat16 [32, 32], replicated, may hold values from -1 to 1
- conv_w: bfloat16 [27, 32, 32], replicated, may hold values from -0.21875 to 0.21875
- cotangent: bfloat16 [4, 32, 12288], P('rep', None, 'slab'), may hold values from -6 to 6
Outputs:
- potential: bfloat16 [4, 32, 12288], P('rep', None, 'slab')
- grad_feats: bfloat16 [4, 32, 12288], P('rep', None, 'slab')
- grad_conv: float32 [27, 32, 32], replicated
- grad_mix: float32 [32, 32], replicated
The draws below stay inside these ranges and needn't reach their ends.
Inputs may be any that keep to these rules, and one draw needn't show every extreme that they name: The first tile_live slots of a slab's list are live, the rest are ignored; in every system some slab has all 96 slots live. `tile_atom`: atom block within the tile's own slab. `tile_cell`: cell block within the slab's window of 8 planes that starts 2 planes below the slab.
All inputs are finite; a program needn't handle non-finite values.
Results may differ from the reference program's by a relative error of at most 0.013.
Values may be sent and summed in bfloat16 or wider, within the bound.
No kernel may reach another device: no remote copies, remote signals or barrier semaphores. Data moves between devices by JAX's collectives and lax.ppermute only.
A program may use at most 128 MiB of HBM per device.

```python
import math
import jax
import jax.numpy as jnp
from jax import lax

C = 32
GY = 32
GX = 64
ZD = 4
ZH = 2
A_DEV = 1536
TILES_DEV = 96
TILE_A = 64
TILE_C = 512
SYSTEMS = 4
SLABS = 8
NZ = 32
ATOMS = 12288
TILES = 768
PW = 8
NB = 32
NAB = 24


def draw_tile_live(key, part):
    first_key, second_key = jax.random.split(jax.random.fold_in(key, 7))
    counts = jax.random.randint(first_key, (SYSTEMS, SLABS), TILES_DEV // 4, TILES_DEV + 1)
    chosen = jax.random.randint(second_key, (SYSTEMS, 1), 0, SLABS)
    slab_ids = jnp.arange(SLABS, dtype=jnp.int32)[None, :]
    return jnp.where(slab_ids == chosen, TILES_DEV, counts).astype(jnp.int32)


def place_ends(array, rng, low, largest):
    index_at = [jax.random.randint(jax.random.fold_in(rng, axis), (), 0, length) for axis, length in enumerate(array.shape)]
    longest = array.shape.index(max(array.shape))
    beside = index_at[:longest] + [(index_at[longest] + 1) % array.shape[longest]] + index_at[longest + 1:]
    return array.at[tuple(index_at)].set(low).at[tuple(beside)].set(largest)


def shard_levels(own_key, extent, cuts, smallest, top_value):
    loudness, own = 1.0, jax.random.fold_in(own_key, 6)
    for dim, blocks in cuts:
        draws = jnp.exp(jax.random.uniform(jax.random.fold_in(own, dim), (blocks,), jnp.float32, smallest / len(cuts), top_value / len(cuts)))
        loudness = loudness * jnp.repeat(draws, extent[dim] // blocks).reshape([-1 if axis == dim else 1 for axis in range(len(extent))])
    return loudness


def normal_values(rng, dims, scale, limit, shards=(), kind=jnp.bfloat16):
    factor_of = shard_levels(rng, dims, shards, -0.22, 0.18) if shards else 1.0
    values = jax.random.normal(rng, dims, jnp.float32) * scale * factor_of
    return jnp.minimum(jnp.maximum(values, -limit), limit).astype(kind)


def setup_inputs(seed: int = 0) -> dict:
    streams_of = jax.random.split(jax.random.key(seed), 9)
    feats = normal_values(streams_of[0], (SYSTEMS, C, ATOMS), 1.0, 6.0, ((0, 4), (2, 8)))
    tile_weight = normal_values(streams_of[1], (SYSTEMS, TILES, TILE_A, TILE_C), TILE_C ** -0.5, 0.25, ((0, 4), (1, 8)))
    tile_atom = place_ends(jax.random.randint(streams_of[2], (SYSTEMS, TILES), 0, NAB), jax.random.fold_in(streams_of[2], 1), 0, NAB - 1).astype(jnp.int32)
    tile_cell = place_ends(jax.random.randint(streams_of[3], (SYSTEMS, TILES), 0, NB), jax.random.fold_in(streams_of[3], 1), 0, NB - 1).astype(jnp.int32)
    tile_live = draw_tile_live(jax.random.fold_in(streams_of[8], 71), 0)
    w_mix = normal_values(streams_of[5], (C, C), C ** -0.5, 1.0)
    conv_w = normal_values(streams_of[6], (27, C, C), (27 * C) ** -0.5, 0.21875)
    cotangent = normal_values(streams_of[7], (SYSTEMS, C, ATOMS), 1.0, 6.0, ((0, 4), (2, 8)))
    return dict(feats=feats, tile_weight=tile_weight, tile_atom=tile_atom, tile_cell=tile_cell, tile_live=tile_live, w_mix=w_mix, conv_w=conv_w, cotangent=cotangent)


def shifted_stack(field):
    planes = field.shape[1]
    shaped = field.reshape(C, planes, GY, GX)
    pieces = []
    for row_off in (-1, 0, 1):
        for col_off in (-1, 0, 1):
            rolled = jnp.roll(shaped, (-row_off, -col_off), (2, 3))
            pieces.append(rolled.reshape(C, planes, GY * GX))
    return jnp.concatenate(pieces, axis=0)

def conv_valid(field, kernel_set):
    planes = field.shape[1] - 2
    stacked = shifted_stack(field).astype(jnp.float32)
    result = jnp.zeros((C, planes, GY * GX), jnp.float32)
    for plane_off in range(3):
        kernel = jnp.transpose(kernel_set[plane_off * 9:(plane_off + 1) * 9], (1, 0, 2)).reshape(C, 9 * C)
        result = result + jnp.einsum('ok,kpn->opn', kernel.astype(jnp.float32), stacked[:, plane_off:plane_off + planes])
    return result

def weight_grad(upstream, field):
    planes = upstream.shape[1]
    stacked = shifted_stack(field).astype(jnp.float32)
    collected = []
    for plane_off in range(3):
        product = jnp.einsum('opn,kpn->ok', upstream.astype(jnp.float32), stacked[:, plane_off:plane_off + planes])
        collected.append(jnp.transpose(product.reshape(C, 9, C), (1, 0, 2)))
    return jnp.concatenate(collected, axis=0)

def wrap_planes(field, margin):
    return jnp.concatenate([field[:, NZ - margin:], field, field[:, :margin]], axis=1)

def deposit_slab(source, weights, atom_ids, cell_ids, live_tiles):
    blocks = source.reshape(C, NAB, TILE_A)
    picked = blocks[:, atom_ids]
    product = jnp.einsum('ctk,tkn->tcn', picked.astype(jnp.float32), weights.astype(jnp.float32))
    alive = jnp.arange(TILES_DEV, dtype=jnp.int32) < live_tiles
    product = jnp.where(alive[:, None, None], product, 0.0)
    sums = jax.ops.segment_sum(product, cell_ids, num_segments=NB)
    return jnp.transpose(sums, (1, 0, 2)).reshape(C, PW, GY * GX)

def collect_slab(window, weights, atom_ids, cell_ids, live_tiles):
    blocks = window.reshape(C, NB, TILE_C)
    picked = blocks[:, cell_ids]
    product = jnp.einsum('ctn,tkn->tck', picked.astype(jnp.float32), weights.astype(jnp.float32))
    alive = jnp.arange(TILES_DEV, dtype=jnp.int32) < live_tiles
    product = jnp.where(alive[:, None, None], product, 0.0)
    sums = jax.ops.segment_sum(product, atom_ids, num_segments=NAB)
    return jnp.transpose(sums, (1, 0, 2)).reshape(C, A_DEV)

def spread_mesh(source, weights, atom_ids, cell_ids, live_counts):
    slab_src = jnp.transpose(source.reshape(C, SLABS, A_DEV), (1, 0, 2))
    slab_w = weights.reshape(SLABS, TILES_DEV, TILE_A, TILE_C)
    slab_a = atom_ids.reshape(SLABS, TILES_DEV)
    slab_c = cell_ids.reshape(SLABS, TILES_DEV)
    padded = jnp.zeros((C, NZ + 2 * ZH, GY * GX), jnp.float32)

    def one_slab(carry, inputs):
        slab_index, src_part, w_part, a_part, c_part, live_part = inputs
        window = deposit_slab(src_part, w_part, a_part, c_part, live_part)
        offset = (slab_index * ZD).astype(jnp.int32)
        current = lax.dynamic_slice_in_dim(carry, offset, PW, 1)
        return (lax.dynamic_update_slice_in_dim(carry, current + window, offset, 1), None)
    padded, _ = lax.scan(one_slab, padded, (jnp.arange(SLABS, dtype=jnp.int32), slab_src, slab_w, slab_a, slab_c, live_counts))
    mesh = padded[:, ZH:ZH + NZ]
    mesh = mesh.at[:, :ZH].add(padded[:, NZ + ZH:])
    mesh = mesh.at[:, NZ - ZH:].add(padded[:, :ZH])
    return mesh

def gather_atoms(mesh, weights, atom_ids, cell_ids, live_counts):
    extended = wrap_planes(mesh, ZH)
    slab_w = weights.reshape(SLABS, TILES_DEV, TILE_A, TILE_C)
    slab_a = atom_ids.reshape(SLABS, TILES_DEV)
    slab_c = cell_ids.reshape(SLABS, TILES_DEV)

    def one_slab(inputs):
        slab_index, w_part, a_part, c_part, live_part = inputs
        offset = (slab_index * ZD).astype(jnp.int32)
        window = lax.dynamic_slice_in_dim(extended, offset, PW, 1)
        return collect_slab(window, w_part, a_part, c_part, live_part)
    result = lax.map(one_slab, (jnp.arange(SLABS, dtype=jnp.int32), slab_w, slab_a, slab_c, live_counts))
    return jnp.transpose(result, (1, 0, 2)).reshape(C, ATOMS)

def reference(feats, tile_weight, tile_atom, tile_cell, tile_live, w_mix, conv_w, cotangent):
    kernel_flip = jnp.transpose(conv_w[::-1], (0, 2, 1))

    def one_system(inputs):
        atom_feats, weights, atom_ids, cell_ids, live_counts, upstream = inputs
        mixed = jnp.dot(w_mix, atom_feats, preferred_element_type=jnp.float32).astype(jnp.bfloat16)
        density = spread_mesh(mixed, weights, atom_ids, cell_ids, live_counts).astype(jnp.bfloat16)
        field_mesh = conv_valid(wrap_planes(density, 1), conv_w).astype(jnp.bfloat16)
        potential = gather_atoms(field_mesh, weights, atom_ids, cell_ids, live_counts).astype(jnp.bfloat16)
        mesh_grad = spread_mesh(upstream, weights, atom_ids, cell_ids, live_counts).astype(jnp.bfloat16)
        conv_part = weight_grad(mesh_grad, wrap_planes(density, 1))
        density_grad = conv_valid(wrap_planes(mesh_grad, 1), kernel_flip).astype(jnp.bfloat16)
        mixed_grad = gather_atoms(density_grad, weights, atom_ids, cell_ids, live_counts).astype(jnp.bfloat16)
        feats_grad = jnp.dot(w_mix.T, mixed_grad, preferred_element_type=jnp.float32).astype(jnp.bfloat16)
        mix_part = jnp.dot(mixed_grad, atom_feats.T, preferred_element_type=jnp.float32)
        return (potential, feats_grad, conv_part, mix_part)
    potential, feats_grad, conv_parts, mix_parts = lax.map(one_system, (feats, tile_weight, tile_atom, tile_cell, tile_live, cotangent))
    grad_conv = lax.optimization_barrier(jnp.sum(conv_parts, axis=0)) / math.sqrt(SYSTEMS * NZ * GY * GX)
    grad_mix = lax.optimization_barrier(jnp.sum(mix_parts, axis=0)) / math.sqrt(SYSTEMS * ATOMS)
    return (potential, feats_grad, grad_conv, grad_mix)
```

```python
import functools
import math

import jax
import jax.numpy as jnp
from jax import lax
from jax.experimental import pallas as pl
from jax.experimental.pallas import tpu as pltpu
from jax.sharding import PartitionSpec as P

GY = 32
GX = 64
ZD = 4
ZH = 2
F32 = jnp.float32
BF16 = jnp.bfloat16
VMEM_LIMIT = 40 * 1024 * 1024


def params(*semantics):
    return pltpu.CompilerParams(
        dimension_semantics=semantics or None, vmem_limit_bytes=VMEM_LIMIT
    )


def whole():
    return pl.BlockSpec(memory_space=pltpu.VMEM)


def deposit_kernel(
    atom_ref, cell_ref, live_ref, feats_ref, cot_ref, weight_ref,
    dd_ref, dm_ref, du_ref, ed_ref, em_ref, eu_ref, source, total,
):
    step = pl.program_id(0)
    channels = feats_ref.shape[0]
    tiles, tile_a, tile_c = weight_ref.shape
    quarters = GY * GX // tile_c

    @pl.when(step == 0)
    def _():
        for a in range(source.shape[0]):
            cols = slice(a * tile_a, (a + 1) * tile_a)
            source[a, :channels] = feats_ref[:, cols]
            source[a, channels:] = cot_ref[:, cols]
        total[...] = jnp.zeros_like(total)

    for j in range(tiles):
        slot = step * tiles + j
        picked = source[atom_ref[slot]]
        picked = jnp.where(slot < live_ref[0], picked, jnp.zeros_like(picked))
        total[cell_ref[slot]] += jnp.dot(
            picked, weight_ref[j], preferred_element_type=F32
        )

    @pl.when(step == pl.num_programs(0) - 1)
    def _():
        first = 0
        for d_ref, e_ref in ((dd_ref, ed_ref), (dm_ref, em_ref), (du_ref, eu_ref)):
            count = d_ref.shape[0]
            d_ref[...] = total[first : first + count, :channels].astype(BF16)
            e_ref[...] = total[first : first + count, channels:].astype(BF16)
            first += count


def deposit(feats, cot, weights, atom_ids, cell_ids, live):
    channels, atoms = feats.shape
    tiles, tile_a, tile_c = weights.shape
    per_step = 8
    quarters = GY * GX // tile_c
    rim = (ZH + 1) * quarters
    middle = (ZD - 2) * quarters
    shapes = []
    for _ in range(2):
        for count in (rim, middle, rim):
            shapes.append(jax.ShapeDtypeStruct((count, channels, tile_c), BF16))
    blocks = (ZD + 2 * ZH) * quarters
    return pl.pallas_call(
        deposit_kernel,
        grid_spec=pltpu.PrefetchScalarGridSpec(
            num_scalar_prefetch=3,
            grid=(tiles // per_step,),
            in_specs=[
                whole(),
                whole(),
                pl.BlockSpec((per_step, tile_a, tile_c), lambda i, *_: (i, 0, 0)),
            ],
            out_specs=[whole()] * 6,
            scratch_shapes=[
                pltpu.VMEM((atoms // tile_a, 2 * channels, tile_a), BF16),
                pltpu.VMEM((blocks, 2 * channels, tile_c), F32),
            ],
        ),
        out_shape=shapes,
        compiler_params=params("arbitrary"),
        name="deposit",
    )(atom_ids, cell_ids, live, feats, cot, weights)


def toeplitz_kernel(conv_ref, forward_ref, backward_ref):
    channels = conv_ref.shape[1]
    for flip, out_ref in ((False, forward_ref), (True, backward_ref)):
        for dx in range(3):
            for dy in range(3):
                parts = []
                for dz in range(3):
                    if flip:
                        k = 9 * (2 - dz) + 3 * (2 - dy) + (2 - dx)
                        parts.append(conv_ref[k].astype(F32).T)
                    else:
                        parts.append(conv_ref[9 * dz + 3 * dy + dx].astype(F32))
                band = jnp.concatenate(parts, axis=1)
                for po in range(ZD):
                    pieces = []
                    if po:
                        pieces.append(jnp.zeros((channels, po * channels), F32))
                    pieces.append(band)
                    rest = (ZD - 1 - po) * channels
                    if rest:
                        pieces.append(jnp.zeros((channels, rest), F32))
                    row = (dy * ZD + po) * channels
                    out_ref[dx, row : row + channels] = jnp.concatenate(
                        pieces, axis=1
                    ).astype(BF16)


def toeplitz(conv_w):
    channels = conv_w.shape[1]
    shape = jax.ShapeDtypeStruct((3, 3 * ZD * channels, (ZD + 2) * channels), BF16)
    return pl.pallas_call(
        toeplitz_kernel,
        in_specs=[whole()],
        out_specs=[whole()] * 2,
        out_shape=[shape, shape],
        compiler_params=params(),
        name="toeplitz",
    )(conv_w)


def joined_planes(down, middle, up, from_below, from_above):
    quarters = middle.shape[0] // (ZD - 2)
    own = [down[q] for q in range(quarters, 3 * quarters)]
    own += [middle[q] for q in range(2 * quarters)]
    own += [up[q] for q in range(2 * quarters)]
    other = [from_below[q] for q in range(3 * quarters)]
    other += [from_above[q] for q in range(3 * quarters)]
    sums = [a.astype(F32) + b.astype(F32) for a, b in zip(own, other)]
    return [
        jnp.concatenate(sums[p * quarters : (p + 1) * quarters], axis=1)
        for p in range(ZD + 2)
    ]


def column(shape):
    return lax.rem(lax.broadcasted_iota(jnp.int32, shape, 1), GX)


def store_shifted(out_ref, row, value):
    rows, cells = value.shape
    x = column(value.shape)
    group = out_ref.shape[0] // 3
    left = jnp.where(
        x == 0, pltpu.roll(value, cells - GX + 1, 1), pltpu.roll(value, 1, 1)
    )
    right = jnp.where(
        x == GX - 1, pltpu.roll(value, GX - 1, 1), pltpu.roll(value, cells - 1, 1)
    )
    out_ref[row : row + rows] = left.astype(BF16)
    out_ref[group + row : group + row + rows] = value.astype(BF16)
    out_ref[2 * group + row : 2 * group + row + rows] = right.astype(BF16)


def conv_planes(matrix_ref, shifted, partial, low_ref, high_ref):
    cells = shifted.shape[1]
    group = shifted.shape[0] // 3
    chunk = low_ref.shape[2]
    for q in range(cells // chunk):
        cols = slice(q * chunk, (q + 1) * chunk)
        acc = None
        for dx in range(3):
            term = jnp.dot(
                matrix_ref[dx],
                shifted[dx * group : (dx + 1) * group, cols],
                preferred_element_type=F32,
            )
            acc = term if acc is None else acc + term
        partial[:, cols] = acc
    channels = low_ref.shape[1]
    quarters = cells // chunk
    for po in range(ZD):
        rows = slice(po * channels, (po + 1) * channels)
        third = ZD * channels
        before = partial[rows, :]
        here = partial[third + po * channels : third + (po + 1) * channels, :]
        after = partial[2 * third + po * channels : 2 * third + (po + 1) * channels, :]
        result = (
            here + pltpu.roll(before, GX, 1) + pltpu.roll(after, cells - GX, 1)
        ).astype(BF16)
        out_ref = low_ref if po < ZH else high_ref
        first = (po % ZH) * quarters
        for q in range(quarters):
            out_ref[first + q] = result[:, q * chunk : (q + 1) * chunk]


def forward_kernel(
    down, middle, up, below, above, mix_ref, matrix_ref,
    low_ref, high_ref, plain_ref, shifted, partial,
):
    channels = mix_ref.shape[0]
    for p, plane in enumerate(joined_planes(down, middle, up, below, above)):
        plane = plane.astype(BF16)
        plain_ref[p * channels : (p + 1) * channels] = plane
        mixed = jnp.dot(mix_ref[...], plane, preferred_element_type=F32)
        store_shifted(shifted, p * channels, mixed.astype(BF16).astype(F32))
    conv_planes(matrix_ref, shifted, partial, low_ref, high_ref)


def backward_kernel(
    down, middle, up, below, above, matrix_ref, plain_ref,
    low_ref, high_ref, grad_ref, shifted, partial, upstream,
):
    channels = low_ref.shape[1]
    cells = plain_ref.shape[1]
    for p in range(ZD + 2):
        rows = slice(p * channels, (p + 1) * channels)
        store_shifted(shifted, p * channels, plain_ref[rows].astype(F32))
    planes = joined_planes(down, middle, up, below, above)
    third = ZD * channels
    for p in range(ZD):
        plane = planes[p + 1]
        row = p * channels
        upstream[row : row + channels] = pltpu.roll(plane, cells - GX, 1).astype(BF16)
        upstream[third + row : third + row + channels] = plane.astype(BF16)
        upstream[2 * third + row : 2 * third + row + channels] = pltpu.roll(
            plane, GX, 1
        ).astype(BF16)
    wide = (ZD + 2) * channels
    for dx in range(3):
        product = lax.dot_general(
            upstream[...],
            shifted[dx * wide : (dx + 1) * wide],
            (((1,), (1,)), ((), ())),
            preferred_element_type=F32,
        )
        for dy in range(3):
            block = None
            for po in range(ZD):
                row = (dy * ZD + po) * channels
                piece = product[
                    row : row + channels, po * channels : (po + 3) * channels
                ]
                block = piece if block is None else block + piece
            row = (3 * dy + dx) * channels
            grad_ref[row : row + channels] = jnp.concatenate(
                [block, jnp.zeros((channels, channels), F32)], axis=1
            )
    for p, plane in enumerate(planes):
        store_shifted(shifted, p * channels, plane.astype(BF16).astype(F32))
    conv_planes(matrix_ref, shifted, partial, low_ref, high_ref)


def gather_kernel(
    atom_ref, cell_ref, live_ref, weight_ref, mix_ref,
    a0, a1, a2, a3, b0, b1, b2, b3, potential_ref, grad_ref, field, total,
):
    step = pl.program_id(0)
    channels = mix_ref.shape[0]
    tiles, tile_a, tile_c = weight_ref.shape

    @pl.when(step == 0)
    def _():
        first = 0
        for a, b in ((a0, b0), (a1, b1), (a2, b2), (a3, b3)):
            count = a.shape[0]
            field[first : first + count, :channels] = a[...]
            field[first : first + count, channels:] = b[...]
            first += count
        total[...] = jnp.zeros_like(total)

    for j in range(tiles):
        slot = step * tiles + j
        product = lax.dot_general(
            field[cell_ref[slot]],
            weight_ref[j],
            (((1,), (1,)), ((), ())),
            preferred_element_type=F32,
        )
        total[atom_ref[slot]] += jnp.where(
            slot < live_ref[0], product, jnp.zeros_like(product)
        )

    @pl.when(step == pl.num_programs(0) - 1)
    def _():
        mix_t = mix_ref[...].astype(F32).T.astype(BF16)
        for a in range(0, total.shape[0], 2):
            pair = jnp.concatenate([total[a], total[a + 1]], axis=1).astype(BF16)
            cols = slice(a * tile_a, (a + 2) * tile_a)
            potential_ref[:, cols] = pair[:channels]
            grad_ref[:, cols] = jnp.dot(
                mix_t, pair[channels:], preferred_element_type=F32
            ).astype(BF16)


def gather(phi, drho, weights, atom_ids, cell_ids, live, w_mix, atoms):
    tiles, tile_a, tile_c = weights.shape
    channels = w_mix.shape[0]
    per_step = 8
    blocks = sum(part.shape[0] for part in phi)
    shape = jax.ShapeDtypeStruct((channels, atoms), BF16)
    return pl.pallas_call(
        gather_kernel,
        grid_spec=pltpu.PrefetchScalarGridSpec(
            num_scalar_prefetch=3,
            grid=(tiles // per_step,),
            in_specs=[
                pl.BlockSpec((per_step, tile_a, tile_c), lambda i, *_: (i, 0, 0)),
            ]
            + [whole()] * 9,
            out_specs=[whole()] * 2,
            scratch_shapes=[
                pltpu.VMEM((blocks, 2 * channels, tile_c), BF16),
                pltpu.VMEM((atoms // tile_a, 2 * channels, tile_a), F32),
            ],
        ),
        out_shape=[shape, shape],
        compiler_params=params("arbitrary"),
        name="gather",
    )(atom_ids, cell_ids, live, weights, w_mix, *phi, *drho)


def finish_kernel(total_ref, mix_ref, conv_ref, conv_out, mix_out, *, conv_scale, mix_scale):
    channels = mix_ref.shape[0]
    mix = mix_ref[...].astype(F32)
    acc = jnp.zeros((channels, channels), F32)
    for dy in range(3):
        for dx in range(3):
            row = (3 * dy + dx) * channels
            block = total_ref[row : row + channels]
            for dz in range(3):
                k = 9 * dz + 3 * dy + dx
                part = block[:, dz * channels : (dz + 1) * channels]
                conv_out[k] = lax.dot_general(
                    part, mix, (((1,), (1,)), ((), ())),
                    precision=lax.Precision.HIGHEST, preferred_element_type=F32,
                ) * (1.0 / conv_scale)
                acc = acc + lax.dot_general(
                    conv_ref[k].astype(F32), part, (((0,), (0,)), ((), ())),
                    precision=lax.Precision.HIGHEST, preferred_element_type=F32,
                )
    mix_out[...] = acc * (1.0 / mix_scale)


def ring(value, axis, steps):
    count = lax.axis_size(axis)
    pairs = [(source, (source + steps) % count) for source in range(count)]
    return lax.ppermute(value, axis, pairs)


def reduced(value):
    for axis in ("slab", "rep"):
        count = lax.axis_size(axis)
        stride = 1
        while stride < count:
            pairs = [(source, source ^ stride) for source in range(count)]
            value = value + lax.ppermute(value, axis, pairs)
            stride *= 2
    return value


def local(feats, tile_weight, tile_atom, tile_cell, tile_live, w_mix, conv_w, cotangent):
    feats, weights, cot = feats[0], tile_weight[0], cotangent[0]
    atom_ids, cell_ids, live = tile_atom[0], tile_cell[0], tile_live[0]
    channels, atoms = feats.shape
    tile_c = weights.shape[2]
    quarters = GY * GX // tile_c
    cells = GY * GX

    dd, dm, du, ed, em, eu = deposit(feats, cot, weights, atom_ids, cell_ids, live)
    d_below, d_above = ring(du, "slab", 1), ring(dd, "slab", -1)
    e_below, e_above = ring(eu, "slab", 1), ring(ed, "slab", -1)
    forward, backward = toeplitz(conv_w)

    half = jax.ShapeDtypeStruct((ZH * quarters, channels, tile_c), BF16)
    rows = (ZD + 2) * channels
    scratch = [
        pltpu.VMEM((3 * rows, cells), BF16),
        pltpu.VMEM((3 * ZD * channels, cells), F32),
    ]
    phi_low, phi_high, plain = pl.pallas_call(
        forward_kernel,
        in_specs=[whole()] * 7,
        out_specs=[whole()] * 3,
        out_shape=[half, half, jax.ShapeDtypeStruct((rows, cells), BF16)],
        scratch_shapes=scratch,
        compiler_params=params(),
        name="forward",
    )(dd, dm, du, d_below, d_above, w_mix, forward)
    phi_below, phi_above = ring(phi_high, "slab", 1), ring(phi_low, "slab", -1)

    drho_low, drho_high, grads = pl.pallas_call(
        backward_kernel,
        in_specs=[whole()] * 7,
        out_specs=[whole()] * 3,
        out_shape=[half, half, jax.ShapeDtypeStruct((9 * channels, 4 * channels), F32)],
        scratch_shapes=scratch + [pltpu.VMEM((3 * ZD * channels, cells), BF16)],
        compiler_params=params(),
        name="backward",
    )(ed, em, eu, e_below, e_above, backward, plain)
    drho_below, drho_above = ring(drho_high, "slab", 1), ring(drho_low, "slab", -1)

    groups = lax.axis_size("rep") * lax.axis_size("slab")
    total = reduced(grads)
    conv_grad, mix_grad = pl.pallas_call(
        functools.partial(
            finish_kernel,
            conv_scale=math.sqrt(groups * ZD * cells),
            mix_scale=math.sqrt(groups * atoms),
        ),
        in_specs=[whole()] * 3,
        out_specs=[whole()] * 2,
        out_shape=[
            jax.ShapeDtypeStruct(conv_w.shape, F32),
            jax.ShapeDtypeStruct(w_mix.shape, F32),
        ],
        compiler_params=params(),
        name="finish",
    )(total, w_mix, conv_w)

    potential, feats_grad = gather(
        (phi_below, phi_low, phi_high, phi_above),
        (drho_below, drho_low, drho_high, drho_above),
        weights, atom_ids, cell_ids, live, w_mix, atoms,
    )
    return potential[None], feats_grad[None], conv_grad, mix_grad


def solution(mesh):
    return jax.shard_map(
        local,
        mesh=mesh,
        in_specs=(
            P("rep", None, "slab"),
            P("rep", "slab", None, None),
            P("rep", "slab"),
            P("rep", "slab"),
            P("rep", "slab"),
            P(),
            P(),
            P("rep", None, "slab"),
        ),
        out_specs=(P("rep", None, "slab"), P("rep", None, "slab"), P(), P()),
        check_vma=False,
    )
```

```python
import functools
import math

import jax
import jax.numpy as jnp
from jax import lax
from jax.experimental import pallas as pl
from jax.experimental.pallas import tpu as pltpu
from jax.sharding import PartitionSpec as P

GY = 32
GX = 64
ZD = 4
ZH = 2
F32 = jnp.float32
BF16 = jnp.bfloat16
VMEM_LIMIT = 16 * 1024 * 1024


def params(*semantics):
    return pltpu.CompilerParams(
        dimension_semantics=semantics or None, vmem_limit_bytes=VMEM_LIMIT
    )


def whole():
    return pl.BlockSpec(memory_space=pltpu.VMEM)


def copies(pairs, sems):
    return [
        pltpu.make_async_copy(source, target, sems.at[i])
        for i, (source, target) in enumerate(pairs)
    ]


def add_tiles(tiles, atom_ref, cell_ref, live, source, weight_ref, total):
    for j in range(tiles.start, tiles.stop):
        picked = source[atom_ref[0, j]]
        picked = jnp.where(j < live, picked, jnp.zeros_like(picked))
        total[cell_ref[0, j]] += jnp.dot(
            picked, weight_ref[j], preferred_element_type=F32
        )


def split_atoms(field, source):
    tile_a = source.shape[2]
    for a in range(source.shape[0]):
        source[a] = field[:, a * tile_a : (a + 1) * tile_a]


def write_parts(total, refs):
    first = 0
    for ref in refs:
        count = ref.shape[0]
        ref[...] = total[first : first + count].astype(BF16)
        first += count


def first_deposit_kernel(
    atom_hbm, cell_hbm, live_ref, feats_hbm, weight_hbm,
    down_ref, middle_ref, up_ref, weight_ref,
    atom_ref, cell_ref, small_sems, source, total, feats, weight_sems,
):
    chunks = weight_sems.shape[0]
    per_chunk = weight_ref.shape[0] // chunks
    small = copies(
        ((atom_hbm, atom_ref), (cell_hbm, cell_ref), (feats_hbm, feats)), small_sems
    )
    parts = [slice(i * per_chunk, (i + 1) * per_chunk) for i in range(chunks)]
    large = copies([(weight_hbm.at[p], weight_ref.at[p]) for p in parts], weight_sems)
    for copy in small + large:
        copy.start()
    total[...] = jnp.zeros_like(total)
    for copy in small:
        copy.wait()
    split_atoms(feats[...], source)
    live = live_ref[0, 0]
    for part, copy in zip(parts, large):
        copy.wait()
        add_tiles(part, atom_ref, cell_ref, live, source, weight_ref, total)
    write_parts(total, (down_ref, middle_ref, up_ref))


def second_deposit_kernel(
    atom_hbm, cell_hbm, live_ref, cot_ref, weight_ref,
    down_ref, middle_ref, up_ref,
    atom_ref, cell_ref, small_sems, source, total,
):
    small = copies(((atom_hbm, atom_ref), (cell_hbm, cell_ref)), small_sems)
    for copy in small:
        copy.start()
    total[...] = jnp.zeros_like(total)
    split_atoms(cot_ref[...], source)
    for copy in small:
        copy.wait()
    tiles = slice(0, weight_ref.shape[0])
    add_tiles(tiles, atom_ref, cell_ref, live_ref[0, 0], source, weight_ref, total)
    write_parts(total, (down_ref, middle_ref, up_ref))


def in_hbm(*values):
    return [pltpu.with_memory_space_constraint(value, pltpu.HBM) for value in values]


def hbm():
    return pl.BlockSpec(memory_space=pltpu.HBM)


def list_scratch(atom_ids, cell_ids):
    return [
        pltpu.SMEM(atom_ids.shape, jnp.int32),
        pltpu.SMEM(cell_ids.shape, jnp.int32),
        pltpu.SemaphoreType.DMA((3,)),
    ]


def list_specs():
    return [hbm(), hbm(), pl.BlockSpec(memory_space=pltpu.SMEM)]


def deposit_shapes(field, weights):
    channels, atoms = field.shape
    _, tile_a, tile_c = weights.shape
    quarters = GY * GX // tile_c
    parts = [
        jax.ShapeDtypeStruct((planes * quarters, channels, tile_c), BF16)
        for planes in (ZH + 1, ZD - 2, ZH + 1)
    ]
    scratch = [
        pltpu.VMEM((atoms // tile_a, channels, tile_a), BF16),
        pltpu.VMEM(((ZD + 2 * ZH) * quarters, channels, tile_c), F32),
    ]
    return parts, scratch


def first_deposit(feats, weights, atom_ids, cell_ids, live):
    parts, scratch = deposit_shapes(feats, weights)
    return pl.pallas_call(
        first_deposit_kernel,
        in_specs=list_specs() + [hbm()] * 2,
        out_specs=[whole()] * 4,
        out_shape=parts + [jax.ShapeDtypeStruct(weights.shape, BF16)],
        scratch_shapes=list_scratch(atom_ids, cell_ids)
        + scratch
        + [pltpu.VMEM(feats.shape, BF16), pltpu.SemaphoreType.DMA((8,))],
        compiler_params=params(),
        name="first_deposit",
    )(*in_hbm(atom_ids, cell_ids), live, *in_hbm(feats, weights))


def second_deposit(cot, weights, atom_ids, cell_ids, live):
    parts, scratch = deposit_shapes(cot, weights)
    return pl.pallas_call(
        second_deposit_kernel,
        in_specs=list_specs() + [whole()] * 2,
        out_specs=[whole()] * 3,
        out_shape=parts,
        scratch_shapes=list_scratch(atom_ids, cell_ids) + scratch,
        compiler_params=params(),
        name="second_deposit",
    )(*in_hbm(atom_ids, cell_ids), live, cot, weights)


def toeplitz_kernel(conv_ref, forward_ref, backward_ref):
    channels = conv_ref.shape[1]
    for flip, out_ref in ((False, forward_ref), (True, backward_ref)):
        for dx in range(3):
            for dy in range(3):
                parts = []
                for dz in range(3):
                    if flip:
                        k = 9 * (2 - dz) + 3 * (2 - dy) + (2 - dx)
                        parts.append(conv_ref[k].astype(F32).T)
                    else:
                        parts.append(conv_ref[9 * dz + 3 * dy + dx].astype(F32))
                band = jnp.concatenate(parts, axis=1)
                for po in range(ZD):
                    pieces = []
                    if po:
                        pieces.append(jnp.zeros((channels, po * channels), F32))
                    pieces.append(band)
                    rest = (ZD - 1 - po) * channels
                    if rest:
                        pieces.append(jnp.zeros((channels, rest), F32))
                    row = (dy * ZD + po) * channels
                    out_ref[dx, row : row + channels] = jnp.concatenate(
                        pieces, axis=1
                    ).astype(BF16)


def toeplitz(conv_w):
    channels = conv_w.shape[1]
    shape = jax.ShapeDtypeStruct((3, 3 * ZD * channels, (ZD + 2) * channels), BF16)
    return pl.pallas_call(
        toeplitz_kernel,
        in_specs=[whole()],
        out_specs=[whole()] * 2,
        out_shape=[shape, shape],
        compiler_params=params(),
        name="toeplitz",
    )(conv_w)


def joined_planes(down, middle, up, from_below, from_above):
    quarters = middle.shape[0] // (ZD - 2)
    own = [down[q] for q in range(quarters, 3 * quarters)]
    own += [middle[q] for q in range(2 * quarters)]
    own += [up[q] for q in range(2 * quarters)]
    other = [from_below[q] for q in range(3 * quarters)]
    other += [from_above[q] for q in range(3 * quarters)]
    sums = [a.astype(F32) + b.astype(F32) for a, b in zip(own, other)]
    return [
        jnp.concatenate(sums[p * quarters : (p + 1) * quarters], axis=1)
        for p in range(ZD + 2)
    ]


def column(shape):
    return lax.rem(lax.broadcasted_iota(jnp.int32, shape, 1), GX)


def store_shifted(out_ref, row, value):
    rows, cells = value.shape
    x = column(value.shape)
    group = out_ref.shape[0] // 3
    left = jnp.where(
        x == 0, pltpu.roll(value, cells - GX + 1, 1), pltpu.roll(value, 1, 1)
    )
    right = jnp.where(
        x == GX - 1, pltpu.roll(value, GX - 1, 1), pltpu.roll(value, cells - 1, 1)
    )
    out_ref[row : row + rows] = left.astype(BF16)
    out_ref[group + row : group + row + rows] = value.astype(BF16)
    out_ref[2 * group + row : 2 * group + row + rows] = right.astype(BF16)


def conv_planes(matrix_ref, shifted, partial, low_ref, high_ref):
    cells = shifted.shape[1]
    group = shifted.shape[0] // 3
    chunk = low_ref.shape[2]
    for q in range(cells // chunk):
        cols = slice(q * chunk, (q + 1) * chunk)
        acc = None
        for dx in range(3):
            term = jnp.dot(
                matrix_ref[dx],
                shifted[dx * group : (dx + 1) * group, cols],
                preferred_element_type=F32,
            )
            acc = term if acc is None else acc + term
        partial[:, cols] = acc
    channels = low_ref.shape[1]
    quarters = cells // chunk
    for po in range(ZD):
        rows = slice(po * channels, (po + 1) * channels)
        third = ZD * channels
        before = partial[rows, :]
        here = partial[third + po * channels : third + (po + 1) * channels, :]
        after = partial[2 * third + po * channels : 2 * third + (po + 1) * channels, :]
        result = (
            here + pltpu.roll(before, GX, 1) + pltpu.roll(after, cells - GX, 1)
        ).astype(BF16)
        out_ref = low_ref if po < ZH else high_ref
        first = (po % ZH) * quarters
        for q in range(quarters):
            out_ref[first + q] = result[:, q * chunk : (q + 1) * chunk]


def forward_kernel(
    down, middle, up, below, above, mix_ref, matrix_ref,
    low_ref, high_ref, plain_ref, shifted, partial,
):
    channels = mix_ref.shape[0]
    for p, plane in enumerate(joined_planes(down, middle, up, below, above)):
        plane = plane.astype(BF16)
        plain_ref[p * channels : (p + 1) * channels] = plane
        mixed = jnp.dot(mix_ref[...], plane, preferred_element_type=F32)
        store_shifted(shifted, p * channels, mixed.astype(BF16).astype(F32))
    conv_planes(matrix_ref, shifted, partial, low_ref, high_ref)


def gradient_kernel(
    parity_ref, down, middle, up, below, above, plain_ref,
    keep_ref, send_ref, sums_ref, shifted, upstream,
):
    channels = down.shape[1]
    cells = plain_ref.shape[1]
    for p in range(ZD + 2):
        rows = slice(p * channels, (p + 1) * channels)
        store_shifted(shifted, p * channels, plain_ref[rows].astype(F32))
    planes = joined_planes(down, middle, up, below, above)
    third = ZD * channels
    for p in range(ZD + 2):
        sums_ref[p * channels : (p + 1) * channels] = planes[p].astype(BF16)
    for p in range(ZD):
        plane = planes[p + 1]
        row = p * channels
        upstream[row : row + channels] = pltpu.roll(plane, cells - GX, 1).astype(BF16)
        upstream[third + row : third + row + channels] = plane.astype(BF16)
        upstream[2 * third + row : 2 * third + row + channels] = pltpu.roll(
            plane, GX, 1
        ).astype(BF16)
    wide = (ZD + 2) * channels
    blocks = []
    for dx in range(3):
        product = lax.dot_general(
            upstream[...],
            shifted[dx * wide : (dx + 1) * wide],
            (((1,), (1,)), ((), ())),
            preferred_element_type=F32,
        )
        for dy in range(3):
            block = None
            for po in range(ZD):
                row = (dy * ZD + po) * channels
                piece = product[
                    row : row + channels, po * channels : (po + 3) * channels
                ]
                block = piece if block is None else block + piece
            blocks.append(
                jnp.concatenate([block, jnp.zeros((channels, channels), F32)], axis=1)
            )
    half = keep_ref.shape[0]
    grads = jnp.concatenate(blocks, axis=0)
    first, second = grads[:half], grads[half:]
    odd = parity_ref[0] == 1

    @pl.when(odd)
    def _():
        keep_ref[...] = second
        send_ref[...] = first

    @pl.when(jnp.logical_not(odd))
    def _():
        keep_ref[...] = first
        send_ref[...] = second


def backward_kernel(sums_ref, matrix_ref, low_ref, high_ref, shifted, partial):
    channels = low_ref.shape[1]
    for p in range(ZD + 2):
        rows = slice(p * channels, (p + 1) * channels)
        store_shifted(shifted, p * channels, sums_ref[rows].astype(F32))
    conv_planes(matrix_ref, shifted, partial, low_ref, high_ref)


def gather_kernel(
    atom_hbm, cell_hbm, live_ref, weight_ref, mix_ref,
    a0, a1, a2, a3, b0, b1, b2, b3, potential_ref, grad_ref,
    atom_ref, cell_ref, small_sems, field, total,
):
    channels = mix_ref.shape[0]
    tiles, tile_a, _ = weight_ref.shape
    small = copies(((atom_hbm, atom_ref), (cell_hbm, cell_ref)), small_sems)
    for copy in small:
        copy.start()
    first = 0
    for a, b in ((a0, b0), (a1, b1), (a2, b2), (a3, b3)):
        count = a.shape[0]
        field[first : first + count, :channels] = a[...]
        field[first : first + count, channels:] = b[...]
        first += count
    total[...] = jnp.zeros_like(total)
    for copy in small:
        copy.wait()
    live = live_ref[0, 0]
    for j in range(tiles):
        product = lax.dot_general(
            field[cell_ref[0, j]],
            weight_ref[j],
            (((1,), (1,)), ((), ())),
            preferred_element_type=F32,
        )
        total[atom_ref[0, j]] += jnp.where(j < live, product, jnp.zeros_like(product))

    mix_t = mix_ref[...].astype(F32).T.astype(BF16)
    for a in range(0, total.shape[0], 2):
        pair = jnp.concatenate([total[a], total[a + 1]], axis=1).astype(BF16)
        cols = slice(a * tile_a, (a + 2) * tile_a)
        potential_ref[:, cols] = pair[:channels]
        grad_ref[:, cols] = jnp.dot(
            mix_t, pair[channels:], preferred_element_type=F32
        ).astype(BF16)


def gather(phi, drho, weights, atom_ids, cell_ids, live, w_mix, atoms):
    _, tile_a, tile_c = weights.shape
    channels = w_mix.shape[0]
    blocks = sum(part.shape[0] for part in phi)
    shape = jax.ShapeDtypeStruct((channels, atoms), BF16)
    return pl.pallas_call(
        gather_kernel,
        in_specs=list_specs() + [whole()] * 10,
        out_specs=[whole()] * 2,
        out_shape=[shape, shape],
        scratch_shapes=list_scratch(atom_ids, cell_ids)
        + [
            pltpu.VMEM((blocks, 2 * channels, tile_c), BF16),
            pltpu.VMEM((atoms // tile_a, 2 * channels, tile_a), F32),
        ],
        compiler_params=params(),
        name="gather",
    )(*in_hbm(atom_ids, cell_ids), live, weights, w_mix, *phi, *drho)


def finish_kernel(
    parity_ref, mine_ref, other_ref, mix_ref, conv_ref, conv_out, mix_out,
    *, conv_scale, mix_scale,
):
    channels = mix_ref.shape[0]
    mine, other = mine_ref[...], other_ref[...]
    odd = parity_ref[0] == 1
    total = jnp.concatenate(
        [jnp.where(odd, other, mine), jnp.where(odd, mine, other)], axis=0
    )
    mix = mix_ref[...].astype(F32)
    acc = jnp.zeros((channels, channels), F32)
    for dz in range(3):
        part = total[:, dz * channels : (dz + 1) * channels]
        scaled = lax.dot_general(
            part, mix, (((1,), (1,)), ((), ())),
            precision=lax.Precision.HIGHEST, preferred_element_type=F32,
        ) * (1.0 / conv_scale)
        kernels = []
        for dx in range(3):
            for dy in range(3):
                row = (3 * dx + dy) * channels
                k = 9 * dz + 3 * dy + dx
                conv_out[k] = scaled[row : row + channels]
                kernels.append(conv_ref[k].astype(F32))
        acc = acc + lax.dot_general(
            jnp.concatenate(kernels, axis=0), part, (((0,), (0,)), ((), ())),
            precision=lax.Precision.HIGHEST, preferred_element_type=F32,
        )
    mix_out[...] = acc * (1.0 / mix_scale)


def ring(value, axis, steps):
    count = lax.axis_size(axis)
    pairs = [(source, (source + steps) % count) for source in range(count)]
    return lax.ppermute(value, axis, pairs)


def exchanged(value, axis, stride):
    count = lax.axis_size(axis)
    return lax.ppermute(value, axis, [(i, i ^ stride) for i in range(count)])


def local(feats, tile_weight, tile_atom, tile_cell, tile_live, w_mix, conv_w, cotangent):
    return step(
        feats[0], tile_weight[0], tile_atom, tile_cell, tile_live,
        w_mix, conv_w, cotangent[0],
    )


def step(feats, weights, atom_ids, cell_ids, live, w_mix, conv_w, cot):
    channels, atoms = feats.shape
    tile_c = weights.shape[2]
    quarters = GY * GX // tile_c
    cells = GY * GX
    smem = pl.BlockSpec(memory_space=pltpu.SMEM)
    parity = jnp.reshape(lax.axis_index("slab") % 2, (1,)).astype(jnp.int32)

    dd, dm, du, held = first_deposit(feats, weights, atom_ids, cell_ids, live)
    d_below, d_above = ring(du, "slab", 1), ring(dd, "slab", -1)
    ed, em, eu = second_deposit(cot, held, atom_ids, cell_ids, live)
    e_below, e_above = ring(eu, "slab", 1), ring(ed, "slab", -1)
    forward, backward = toeplitz(conv_w)

    half = jax.ShapeDtypeStruct((ZH * quarters, channels, tile_c), BF16)
    rows = (ZD + 2) * channels
    scratch = [
        pltpu.VMEM((3 * rows, cells), BF16),
        pltpu.VMEM((3 * ZD * channels, cells), F32),
    ]
    phi_low, phi_high, plain = pl.pallas_call(
        forward_kernel,
        in_specs=[whole()] * 7,
        out_specs=[whole()] * 3,
        out_shape=[half, half, jax.ShapeDtypeStruct((rows, cells), BF16)],
        scratch_shapes=scratch,
        compiler_params=params(),
        name="forward",
    )(dd, dm, du, d_below, d_above, w_mix, forward)
    phi_below, phi_above = ring(phi_high, "slab", 1), ring(phi_low, "slab", -1)

    part = jax.ShapeDtypeStruct((9 * channels // 2, 4 * channels), F32)
    keep, send, sums = pl.pallas_call(
        gradient_kernel,
        in_specs=[smem] + [whole()] * 6,
        out_specs=[whole()] * 3,
        out_shape=[part, part, jax.ShapeDtypeStruct((rows, cells), BF16)],
        scratch_shapes=[scratch[0], pltpu.VMEM((3 * ZD * channels, cells), BF16)],
        compiler_params=params(),
        name="gradient",
    )(parity, ed, em, eu, e_below, e_above, plain)
    arrived = exchanged(send, "slab", 1)
    drho_low, drho_high = pl.pallas_call(
        backward_kernel,
        in_specs=[whole()] * 2,
        out_specs=[whole()] * 2,
        out_shape=[half, half],
        scratch_shapes=scratch,
        compiler_params=params(),
        name="backward",
    )(sums, backward)
    drho_below, drho_above = ring(drho_high, "slab", 1), ring(drho_low, "slab", -1)

    total = keep + arrived
    for axis, first in (("rep", 1), ("slab", 4), ("slab", 2)):
        stride = first
        while stride < lax.axis_size(axis) and (axis == "rep" or stride == 2 or stride >= 4):
            arrived = exchanged(total, axis, stride)
            total = total + arrived
            if stride == 2 and axis == "slab":
                break
            stride *= 2
    other = exchanged(total, "slab", 1)

    groups = lax.axis_size("rep") * lax.axis_size("slab")
    conv_grad, mix_grad = pl.pallas_call(
        functools.partial(
            finish_kernel,
            conv_scale=math.sqrt(groups * ZD * cells),
            mix_scale=math.sqrt(groups * atoms),
        ),
        in_specs=[smem] + [whole()] * 4,
        out_specs=[whole()] * 2,
        out_shape=[
            jax.ShapeDtypeStruct(conv_w.shape, F32),
            jax.ShapeDtypeStruct(w_mix.shape, F32),
        ],
        compiler_params=params(),
        name="finish",
    )(parity, total, other, w_mix, conv_w)

    potential, feats_grad = gather(
        (phi_below, phi_low, phi_high, phi_above),
        (drho_below, drho_low, drho_high, drho_above),
        weights, atom_ids, cell_ids, live, w_mix, atoms,
    )
    return potential[None], feats_grad[None], conv_grad, mix_grad


def solution(mesh):
    return jax.shard_map(
        local,
        mesh=mesh,
        in_specs=(
            P("rep", None, "slab"),
            P("rep", "slab", None, None),
            P("rep", "slab"),
            P("rep", "slab"),
            P("rep", "slab"),
            P(),
            P(),
            P("rep", None, "slab"),
        ),
        out_specs=(P("rep", None, "slab"), P("rep", None, "slab"), P(), P()),
        check_vma=False,
    )
```

```python
import functools
import math

import jax
import jax.numpy as jnp
from jax import lax
from jax.experimental import pallas as pl
from jax.experimental.pallas import tpu as pltpu
from jax.sharding import PartitionSpec as P

GY = 32
GX = 64
ZD = 4
ZH = 2
F32 = jnp.float32
BF16 = jnp.bfloat16
VMEM_LIMIT = 16 * 1024 * 1024


def params(*semantics):
    return pltpu.CompilerParams(
        dimension_semantics=semantics or None, vmem_limit_bytes=VMEM_LIMIT
    )


def whole():
    return pl.BlockSpec(memory_space=pltpu.VMEM)


def copies(pairs, sems):
    return [
        pltpu.make_async_copy(source, target, sems.at[i])
        for i, (source, target) in enumerate(pairs)
    ]


def add_tiles(tiles, atom_ref, cell_ref, live, source, weight_ref, total):
    for j in range(tiles.start, tiles.stop):
        picked = source[atom_ref[0, j]]
        picked = jnp.where(j < live, picked, jnp.zeros_like(picked))
        total[cell_ref[0, j]] += jnp.dot(
            picked, weight_ref[j], preferred_element_type=F32
        )


def split_atoms(field, source):
    tile_a = source.shape[2]
    for a in range(source.shape[0]):
        source[a] = field[:, a * tile_a : (a + 1) * tile_a]


def write_parts(total, refs):
    first = 0
    for ref in refs:
        count = ref.shape[0]
        ref[...] = total[first : first + count].astype(BF16)
        first += count


def first_deposit_kernel(
    atom_hbm, cell_hbm, live_ref, feats_hbm, weight_hbm,
    down_ref, middle_ref, up_ref, weight_ref,
    atom_ref, cell_ref, small_sems, source, total, feats, weight_sems,
):
    chunks = weight_sems.shape[0]
    per_chunk = weight_ref.shape[0] // chunks
    small = copies(
        ((atom_hbm, atom_ref), (cell_hbm, cell_ref), (feats_hbm, feats)), small_sems
    )
    parts = [slice(i * per_chunk, (i + 1) * per_chunk) for i in range(chunks)]
    large = copies([(weight_hbm.at[p], weight_ref.at[p]) for p in parts], weight_sems)
    for copy in small + large:
        copy.start()
    total[...] = jnp.zeros_like(total)
    for copy in small:
        copy.wait()
    split_atoms(feats[...], source)
    live = live_ref[0, 0]
    for part, copy in zip(parts, large):
        copy.wait()
        add_tiles(part, atom_ref, cell_ref, live, source, weight_ref, total)
    write_parts(total, (down_ref, middle_ref, up_ref))


def second_deposit_kernel(
    atom_hbm, cell_hbm, live_ref, cot_ref, weight_ref,
    *rest,
):
    *parts, atom_ref, cell_ref, small_sems, source, total = rest
    small = copies(((atom_hbm, atom_ref), (cell_hbm, cell_ref)), small_sems)
    for copy in small:
        copy.start()
    total[...] = jnp.zeros_like(total)
    split_atoms(cot_ref[...], source)
    for copy in small:
        copy.wait()
    tiles = slice(0, weight_ref.shape[0])
    add_tiles(tiles, atom_ref, cell_ref, live_ref[0, 0], source, weight_ref, total)
    write_parts(total, parts)


def in_hbm(*values):
    return [pltpu.with_memory_space_constraint(value, pltpu.HBM) for value in values]


def hbm():
    return pl.BlockSpec(memory_space=pltpu.HBM)


def list_scratch(atom_ids, cell_ids):
    return [
        pltpu.SMEM(atom_ids.shape, jnp.int32),
        pltpu.SMEM(cell_ids.shape, jnp.int32),
        pltpu.SemaphoreType.DMA((3,)),
    ]


def list_specs():
    return [hbm(), hbm(), pl.BlockSpec(memory_space=pltpu.SMEM)]


def deposit_shapes(field, weights, planes_of):
    channels, atoms = field.shape
    _, tile_a, tile_c = weights.shape
    quarters = GY * GX // tile_c
    parts = [
        pltpu.VMEM((planes * quarters, channels, tile_c), BF16)
        for planes in planes_of
    ]
    scratch = [
        pltpu.VMEM((atoms // tile_a, channels, tile_a), BF16),
        pltpu.VMEM(((ZD + 2 * ZH) * quarters, channels, tile_c), F32),
    ]
    return parts, scratch


def first_deposit(feats, weights, atom_ids, cell_ids, live):
    parts, scratch = deposit_shapes(feats, weights, (ZH + 1, ZD - 2, ZH + 1))
    return pl.pallas_call(
        first_deposit_kernel,
        in_specs=list_specs() + [hbm()] * 2,
        out_specs=[whole()] * 4,
        out_shape=parts + [pltpu.VMEM(weights.shape, BF16)],
        scratch_shapes=list_scratch(atom_ids, cell_ids)
        + scratch
        + [pltpu.VMEM(feats.shape, BF16), pltpu.SemaphoreType.DMA((8,))],
        compiler_params=params(),
        name="first_deposit",
    )(*in_hbm(atom_ids, cell_ids), live, *in_hbm(feats, weights))


def second_deposit(cot, weights, atom_ids, cell_ids, live):
    parts, scratch = deposit_shapes(cot, weights, (ZH, 1, ZD - 2, 1, ZH))
    return pl.pallas_call(
        second_deposit_kernel,
        in_specs=list_specs() + [whole()] * 2,
        out_specs=[whole()] * len(parts),
        out_shape=parts,
        scratch_shapes=list_scratch(atom_ids, cell_ids) + scratch,
        compiler_params=params(),
        name="second_deposit",
    )(*in_hbm(atom_ids, cell_ids), live, cot, weights)


def toeplitz_kernel(conv_ref, forward_ref, backward_ref):
    channels = conv_ref.shape[1]
    for flip, out_ref in ((False, forward_ref), (True, backward_ref)):
        for dx in range(3):
            for dy in range(3):
                parts = []
                for dz in range(3):
                    if flip:
                        k = 9 * (2 - dz) + 3 * (2 - dy) + (2 - dx)
                        parts.append(conv_ref[k].astype(F32).T)
                    else:
                        parts.append(conv_ref[9 * dz + 3 * dy + dx].astype(F32))
                band = jnp.concatenate(parts, axis=1)
                for po in range(ZD):
                    pieces = []
                    if po:
                        pieces.append(jnp.zeros((channels, po * channels), F32))
                    pieces.append(band)
                    rest = (ZD - 1 - po) * channels
                    if rest:
                        pieces.append(jnp.zeros((channels, rest), F32))
                    row = (dy * ZD + po) * channels
                    out_ref[dx, row : row + channels] = jnp.concatenate(
                        pieces, axis=1
                    ).astype(BF16)


def toeplitz(conv_w):
    channels = conv_w.shape[1]
    shape = pltpu.VMEM((3, 3 * ZD * channels, (ZD + 2) * channels), BF16)
    return pl.pallas_call(
        toeplitz_kernel,
        in_specs=[whole()],
        out_specs=[whole()] * 2,
        out_shape=[shape, shape],
        compiler_params=params(),
        name="toeplitz",
    )(conv_w)


def joined_planes(own, other, quarters):
    def blocks(pieces):
        return [
            ref[q]
            for ref, first, count in pieces
            for q in range(first * quarters, (first + count) * quarters)
        ]

    sums = [a.astype(F32) + b.astype(F32) for a, b in zip(blocks(own), blocks(other))]
    return [
        jnp.concatenate(sums[i : i + quarters], axis=1)
        for i in range(0, len(sums), quarters)
    ]


def column(shape):
    return lax.rem(lax.broadcasted_iota(jnp.int32, shape, 1), GX)


def store_shifted(out_ref, row, value):
    rows, cells = value.shape
    x = column(value.shape)
    group = out_ref.shape[0] // 3
    left = jnp.where(
        x == 0, pltpu.roll(value, cells - GX + 1, 1), pltpu.roll(value, 1, 1)
    )
    right = jnp.where(
        x == GX - 1, pltpu.roll(value, GX - 1, 1), pltpu.roll(value, cells - 1, 1)
    )
    out_ref[row : row + rows] = left.astype(BF16)
    out_ref[group + row : group + row + rows] = value.astype(BF16)
    out_ref[2 * group + row : 2 * group + row + rows] = right.astype(BF16)


def conv_planes(matrix_ref, shifted, partial, low_ref, high_ref):
    cells = shifted.shape[1]
    group = shifted.shape[0] // 3
    chunk = low_ref.shape[2]
    for q in range(cells // chunk):
        cols = slice(q * chunk, (q + 1) * chunk)
        acc = None
        for dx in range(3):
            term = jnp.dot(
                matrix_ref[dx],
                shifted[dx * group : (dx + 1) * group, cols],
                preferred_element_type=F32,
            )
            acc = term if acc is None else acc + term
        partial[:, cols] = acc
    channels = low_ref.shape[1]
    quarters = cells // chunk
    for po in range(ZD):
        rows = slice(po * channels, (po + 1) * channels)
        third = ZD * channels
        before = partial[rows, :]
        here = partial[third + po * channels : third + (po + 1) * channels, :]
        after = partial[2 * third + po * channels : 2 * third + (po + 1) * channels, :]
        result = (
            here + pltpu.roll(before, GX, 1) + pltpu.roll(after, cells - GX, 1)
        ).astype(BF16)
        out_ref = low_ref if po < ZH else high_ref
        first = (po % ZH) * quarters
        for q in range(quarters):
            out_ref[first + q] = result[:, q * chunk : (q + 1) * chunk]


def forward_kernel(
    down, middle, up, below, above, mix_ref, matrix_ref,
    low_ref, high_ref, plain_ref, shifted, partial,
):
    channels = mix_ref.shape[0]
    quarters = low_ref.shape[0] // ZH
    own = ((down, 1, ZH), (middle, 0, ZD - 2), (up, 0, ZH))
    other = ((below, 0, ZH + 1), (above, 0, ZH + 1))
    for p, plane in enumerate(joined_planes(own, other, quarters)):
        plane = plane.astype(BF16)
        plain_ref[p * channels : (p + 1) * channels] = plane
        mixed = jnp.dot(mix_ref[...], plane, preferred_element_type=F32)
        store_shifted(shifted, p * channels, mixed.astype(BF16).astype(F32))
    conv_planes(matrix_ref, shifted, partial, low_ref, high_ref)


def gradient_kernel(
    low, middle, high, below, above, plain_ref,
    keep_ref, send_ref, sums_ref, shifted, upstream,
):
    channels = low.shape[1]
    quarters = low.shape[0]
    cells = plain_ref.shape[1]
    for p in range(ZD + 2):
        rows = slice(p * channels, (p + 1) * channels)
        store_shifted(shifted, p * channels, plain_ref[rows].astype(F32))
    own = ((low, 0, 1), (middle, 0, ZD - 2), (high, 0, 1))
    planes = joined_planes(own, ((below, 0, ZH), (above, 0, ZH)), quarters)
    third = ZD * channels
    for p, plane in enumerate(planes):
        row = p * channels
        sums_ref[row : row + channels] = plane.astype(BF16)
        upstream[row : row + channels] = pltpu.roll(plane, cells - GX, 1).astype(BF16)
        upstream[third + row : third + row + channels] = plane.astype(BF16)
        upstream[2 * third + row : 2 * third + row + channels] = pltpu.roll(
            plane, GX, 1
        ).astype(BF16)
    wide = (ZD + 2) * channels
    blocks = []
    for dx in range(3):
        product = lax.dot_general(
            upstream[...],
            shifted[dx * wide : (dx + 1) * wide],
            (((1,), (1,)), ((), ())),
            preferred_element_type=F32,
        )
        for dy in range(3):
            block = None
            for po in range(ZD):
                row = (dy * ZD + po) * channels
                piece = product[
                    row : row + channels, po * channels : (po + 3) * channels
                ]
                block = piece if block is None else block + piece
            blocks.append(
                jnp.concatenate([block, jnp.zeros((channels, channels), F32)], axis=1)
            )
    half = keep_ref.shape[0]
    grads = jnp.concatenate(blocks, axis=0)
    first, second = grads[:half], grads[half:]
    odd = lax.rem(lax.axis_index("slab"), 2) == 1

    @pl.when(odd)
    def _():
        keep_ref[...] = second.astype(keep_ref.dtype)
        send_ref[...] = first.astype(send_ref.dtype)

    @pl.when(jnp.logical_not(odd))
    def _():
        keep_ref[...] = first.astype(keep_ref.dtype)
        send_ref[...] = second.astype(send_ref.dtype)


def backward_kernel(
    down, up, below, above, sums_ref, matrix_ref, low_ref, high_ref, shifted, partial
):
    channels = low_ref.shape[1]
    quarters = below.shape[0]
    (first,) = joined_planes(((down, 1, 1),), ((below, 0, 1),), quarters)
    (last,) = joined_planes(((up, 0, 1),), ((above, 0, 1),), quarters)
    store_shifted(shifted, 0, first.astype(BF16).astype(F32))
    for p in range(ZD):
        rows = slice(p * channels, (p + 1) * channels)
        store_shifted(shifted, (p + 1) * channels, sums_ref[rows].astype(F32))
    store_shifted(shifted, (ZD + 1) * channels, last.astype(BF16).astype(F32))
    conv_planes(matrix_ref, shifted, partial, low_ref, high_ref)


def gather_kernel(
    atom_hbm, cell_hbm, live_ref, weight_ref, mix_ref,
    a0, a1, a2, a3, b0, b1, b2, b3, potential_ref, grad_ref,
    atom_ref, cell_ref, small_sems, field, total,
):
    channels = mix_ref.shape[0]
    tiles, tile_a, _ = weight_ref.shape
    small = copies(((atom_hbm, atom_ref), (cell_hbm, cell_ref)), small_sems)
    for copy in small:
        copy.start()
    first = 0
    for a, b in ((a0, b0), (a1, b1), (a2, b2), (a3, b3)):
        count = a.shape[0]
        field[first : first + count, :channels] = a[...]
        field[first : first + count, channels:] = b[...]
        first += count
    total[...] = jnp.zeros_like(total)
    for copy in small:
        copy.wait()
    live = live_ref[0, 0]
    for j in range(tiles):
        product = lax.dot_general(
            field[cell_ref[0, j]],
            weight_ref[j],
            (((1,), (1,)), ((), ())),
            preferred_element_type=F32,
        )
        total[atom_ref[0, j]] += jnp.where(j < live, product, jnp.zeros_like(product))

    mix_t = mix_ref[...].astype(F32).T.astype(BF16)
    for a in range(0, total.shape[0], 2):
        pair = jnp.concatenate([total[a], total[a + 1]], axis=1).astype(BF16)
        cols = slice(a * tile_a, (a + 2) * tile_a)
        potential_ref[:, cols] = pair[:channels]
        grad_ref[:, cols] = jnp.dot(
            mix_t, pair[channels:], preferred_element_type=F32
        ).astype(BF16)


def gather(phi, drho, weights, atom_ids, cell_ids, live, w_mix, atoms):
    _, tile_a, tile_c = weights.shape
    channels = w_mix.shape[0]
    blocks = sum(part.shape[0] for part in phi)
    shape = jax.ShapeDtypeStruct((channels, atoms), BF16)
    return pl.pallas_call(
        gather_kernel,
        in_specs=list_specs() + [whole()] * 10,
        out_specs=[whole()] * 2,
        out_shape=[shape, shape],
        scratch_shapes=list_scratch(atom_ids, cell_ids)
        + [
            pltpu.VMEM((blocks, 2 * channels, tile_c), BF16),
            pltpu.VMEM((atoms // tile_a, 2 * channels, tile_a), F32),
        ],
        compiler_params=params(),
        name="gather",
    )(*in_hbm(atom_ids, cell_ids), live, weights, w_mix, *phi, *drho)


def finish_kernel(
    mine_ref, other_ref, mix_ref, conv_ref, conv_out, mix_out,
    *, conv_scale, mix_scale,
):
    channels = mix_ref.shape[0]
    mine, other = mine_ref[...].astype(F32), other_ref[...].astype(F32)
    odd = lax.rem(lax.axis_index("slab"), 2) == 1
    total = jnp.concatenate(
        [jnp.where(odd, other, mine), jnp.where(odd, mine, other)], axis=0
    )
    mix = mix_ref[...].astype(F32)
    acc = jnp.zeros((channels, channels), F32)
    for dz in range(3):
        part = total[:, dz * channels : (dz + 1) * channels]
        scaled = lax.dot_general(
            part, mix, (((1,), (1,)), ((), ())),
            precision=lax.Precision.HIGHEST, preferred_element_type=F32,
        ) * (1.0 / conv_scale)
        kernels = []
        for dx in range(3):
            for dy in range(3):
                row = (3 * dx + dy) * channels
                k = 9 * dz + 3 * dy + dx
                conv_out[k] = scaled[row : row + channels]
                kernels.append(conv_ref[k].astype(F32))
        acc = acc + lax.dot_general(
            jnp.concatenate(kernels, axis=0), part, (((0,), (0,)), ((), ())),
            precision=lax.Precision.HIGHEST, preferred_element_type=F32,
        )
    mix_out[...] = acc * (1.0 / mix_scale)


def ring(value, axis, steps):
    count = lax.axis_size(axis)
    pairs = [(source, (source + steps) % count) for source in range(count)]
    return pltpu.with_memory_space_constraint(
        lax.ppermute(value, axis, pairs), pltpu.VMEM
    )


def exchanged(value, axis, stride):
    count = lax.axis_size(axis)
    return lax.ppermute(value, axis, [(i, i ^ stride) for i in range(count)])


def local(feats, tile_weight, tile_atom, tile_cell, tile_live, w_mix, conv_w, cotangent):
    return step(
        feats[0], tile_weight[0], tile_atom, tile_cell, tile_live,
        w_mix, conv_w, cotangent[0],
    )


def step(feats, weights, atom_ids, cell_ids, live, w_mix, conv_w, cot):
    channels, atoms = feats.shape
    tile_c = weights.shape[2]
    quarters = GY * GX // tile_c
    cells = GY * GX
    smem = pl.BlockSpec(memory_space=pltpu.SMEM)

    dd, dm, du, held = first_deposit(feats, weights, atom_ids, cell_ids, live)
    d_below, d_above = ring(du, "slab", 1), ring(dd, "slab", -1)
    ed, el, em, eh, eu = second_deposit(cot, held, atom_ids, cell_ids, live)
    e_below, e_above = ring(eu, "slab", 1), ring(ed, "slab", -1)
    f_below, f_above = ring(eh, "slab", 1), ring(el, "slab", -1)
    forward, backward = toeplitz(conv_w)

    half = pltpu.VMEM((ZH * quarters, channels, tile_c), BF16)
    rows = (ZD + 2) * channels
    scratch = [
        pltpu.VMEM((3 * rows, cells), BF16),
        pltpu.VMEM((3 * ZD * channels, cells), F32),
    ]
    phi_low, phi_high, plain = pl.pallas_call(
        forward_kernel,
        in_specs=[whole()] * 7,
        out_specs=[whole()] * 3,
        out_shape=[half, half, pltpu.VMEM((rows, cells), BF16)],
        scratch_shapes=scratch,
        compiler_params=params(),
        name="forward",
    )(dd, dm, du, d_below, d_above, w_mix, forward)
    phi_below, phi_above = ring(phi_high, "slab", 1), ring(phi_low, "slab", -1)

    part = pltpu.VMEM((9 * channels // 2, 4 * channels), BF16)
    keep, send, sums = pl.pallas_call(
        gradient_kernel,
        in_specs=[whole()] * 6,
        out_specs=[whole()] * 3,
        out_shape=[part, part, pltpu.VMEM((ZD * channels, cells), BF16)],
        scratch_shapes=[scratch[0], pltpu.VMEM((3 * ZD * channels, cells), BF16)],
        compiler_params=params(),
        name="gradient",
    )(el, em, eh, e_below, e_above, plain)
    arrived = exchanged(send, "slab", 1)
    drho_low, drho_high = pl.pallas_call(
        backward_kernel,
        in_specs=[whole()] * 6,
        out_specs=[whole()] * 2,
        out_shape=[half, half],
        scratch_shapes=scratch,
        compiler_params=params(),
        name="backward",
    )(ed, eu, f_below, f_above, sums, backward)
    drho_below, drho_above = ring(drho_high, "slab", 1), ring(drho_low, "slab", -1)

    total = keep + arrived
    turns = [("rep", 1 << i) for i in range((lax.axis_size("rep") - 1).bit_length())]
    turns += [
        ("slab", 1 << i)
        for i in reversed(range(1, (lax.axis_size("slab") - 1).bit_length()))
    ]
    for axis, stride in turns:
        arrived = exchanged(total, axis, stride)
        total = total + arrived
    other = exchanged(total, "slab", 1)

    groups = lax.axis_size("rep") * lax.axis_size("slab")
    conv_grad, mix_grad = pl.pallas_call(
        functools.partial(
            finish_kernel,
            conv_scale=math.sqrt(groups * ZD * cells),
            mix_scale=math.sqrt(groups * atoms),
        ),
        in_specs=[whole()] * 4,
        out_specs=[whole()] * 2,
        out_shape=[
            jax.ShapeDtypeStruct(conv_w.shape, F32),
            jax.ShapeDtypeStruct(w_mix.shape, F32),
        ],
        compiler_params=params(),
        name="finish",
    )(total, other, w_mix, conv_w)

    potential, feats_grad = gather(
        (phi_below, phi_low, phi_high, phi_above),
        (drho_below, drho_low, drho_high, drho_above),
        weights, atom_ids, cell_ids, live, w_mix, atoms,
    )
    return potential[None], feats_grad[None], conv_grad, mix_grad


def solution(mesh):
    return jax.shard_map(
        local,
        mesh=mesh,
        in_specs=(
            P("rep", None, "slab"),
            P("rep", "slab", None, None),
            P("rep", "slab"),
            P("rep", "slab"),
            P("rep", "slab"),
            P(),
            P(),
            P("rep", None, "slab"),
        ),
        out_specs=(P("rep", None, "slab"), P("rep", None, "slab"), P(), P()),
        check_vma=False,
    )
```

```python
import functools
import math

import jax
import jax.numpy as jnp
from jax import lax
from jax.experimental import pallas as pl
from jax.experimental.pallas import tpu as pltpu
from jax.sharding import PartitionSpec as P

GY = 32
GX = 64
ZD = 4
ZH = 2
F32 = jnp.float32
BF16 = jnp.bfloat16
VMEM_LIMIT = 16 * 1024 * 1024


def params(*semantics):
    return pltpu.CompilerParams(
        dimension_semantics=semantics or None, vmem_limit_bytes=VMEM_LIMIT
    )


def whole():
    return pl.BlockSpec(memory_space=pltpu.VMEM)


def copies(pairs, sems):
    return [
        pltpu.make_async_copy(source, target, sems.at[i])
        for i, (source, target) in enumerate(pairs)
    ]


def add_tiles(tiles, atom_ref, cell_ref, live, source, weight_ref, total):
    for j in range(tiles.start, tiles.stop):
        picked = source[atom_ref[0, j]]
        picked = jnp.where(j < live, picked, jnp.zeros_like(picked))
        total[cell_ref[0, j]] += jnp.dot(
            picked, weight_ref[j], preferred_element_type=F32
        )


def split_atoms(field, source):
    tile_a = source.shape[2]
    for a in range(source.shape[0]):
        source[a] = field[:, a * tile_a : (a + 1) * tile_a]


def write_parts(total, refs):
    first = 0
    for ref in refs:
        count = ref.shape[0]
        ref[...] = total[first : first + count].astype(BF16)
        first += count


def first_deposit_kernel(
    atom_hbm, cell_hbm, live_ref, feats_hbm, weight_hbm,
    down_ref, middle_ref, up_ref, weight_ref,
    atom_ref, cell_ref, small_sems, source, total, feats, weight_sems,
):
    chunks = weight_sems.shape[0]
    per_chunk = weight_ref.shape[0] // chunks
    small = copies(
        ((atom_hbm, atom_ref), (cell_hbm, cell_ref), (feats_hbm, feats)), small_sems
    )
    parts = [slice(i * per_chunk, (i + 1) * per_chunk) for i in range(chunks)]
    large = copies([(weight_hbm.at[p], weight_ref.at[p]) for p in parts], weight_sems)
    ahead = chunks
    for copy in small + large[:ahead]:
        copy.start()
    total[...] = jnp.zeros_like(total)
    for copy in small:
        copy.wait()
    split_atoms(feats[...], source)
    live = live_ref[0, 0]
    for i, (part, copy) in enumerate(zip(parts, large)):
        copy.wait()
        if i + ahead < chunks:
            large[i + ahead].start()
        add_tiles(part, atom_ref, cell_ref, live, source, weight_ref, total)
    write_parts(total, (down_ref, middle_ref, up_ref))


def second_deposit_kernel(
    atom_hbm, cell_hbm, live_ref, cot_ref, weight_ref,
    *rest,
):
    *parts, atom_ref, cell_ref, small_sems, source, total = rest
    small = copies(((atom_hbm, atom_ref), (cell_hbm, cell_ref)), small_sems)
    for copy in small:
        copy.start()
    total[...] = jnp.zeros_like(total)
    split_atoms(cot_ref[...], source)
    for copy in small:
        copy.wait()
    tiles = slice(0, weight_ref.shape[0])
    add_tiles(tiles, atom_ref, cell_ref, live_ref[0, 0], source, weight_ref, total)
    write_parts(total, parts)


def in_hbm(*values):
    return [pltpu.with_memory_space_constraint(value, pltpu.HBM) for value in values]


def hbm():
    return pl.BlockSpec(memory_space=pltpu.HBM)


def list_scratch(atom_ids, cell_ids):
    return [
        pltpu.SMEM(atom_ids.shape, jnp.int32),
        pltpu.SMEM(cell_ids.shape, jnp.int32),
        pltpu.SemaphoreType.DMA((3,)),
    ]


def list_specs():
    return [hbm(), hbm(), pl.BlockSpec(memory_space=pltpu.SMEM)]


def deposit_shapes(field, weights, planes_of):
    channels, atoms = field.shape
    _, tile_a, tile_c = weights.shape
    quarters = GY * GX // tile_c
    parts = [
        pltpu.VMEM((planes * quarters, channels, tile_c), BF16)
        for planes in planes_of
    ]
    scratch = [
        pltpu.VMEM((atoms // tile_a, channels, tile_a), BF16),
        pltpu.VMEM(((ZD + 2 * ZH) * quarters, channels, tile_c), F32),
    ]
    return parts, scratch


def first_deposit(feats, weights, atom_ids, cell_ids, live):
    parts, scratch = deposit_shapes(feats, weights, (ZH + 1, ZD - 2, ZH + 1))
    return pl.pallas_call(
        first_deposit_kernel,
        in_specs=list_specs() + [hbm()] * 2,
        out_specs=[whole()] * 4,
        out_shape=parts + [pltpu.VMEM(weights.shape, BF16)],
        scratch_shapes=list_scratch(atom_ids, cell_ids)
        + scratch
        + [pltpu.VMEM(feats.shape, BF16), pltpu.SemaphoreType.DMA((8,))],
        compiler_params=params(),
        name="first_deposit",
    )(*in_hbm(atom_ids, cell_ids), live, *in_hbm(feats, weights))


def second_deposit(cot, weights, atom_ids, cell_ids, live):
    parts, scratch = deposit_shapes(cot, weights, (ZH, 1, ZD - 2, 1, ZH))
    return pl.pallas_call(
        second_deposit_kernel,
        in_specs=list_specs() + [whole()] * 2,
        out_specs=[whole()] * len(parts),
        out_shape=parts,
        scratch_shapes=list_scratch(atom_ids, cell_ids) + scratch,
        compiler_params=params(),
        name="second_deposit",
    )(*in_hbm(atom_ids, cell_ids), live, cot, weights)


def toeplitz_kernel(conv_ref, forward_ref, backward_ref):
    channels = conv_ref.shape[1]
    for flip, out_ref in ((False, forward_ref), (True, backward_ref)):
        for dy in range(3):
            bands = []
            for dx in range(3):
                parts = []
                for dz in range(3):
                    if flip:
                        k = 9 * (2 - dz) + 3 * (2 - dy) + (2 - dx)
                        parts.append(conv_ref[k].astype(F32).T)
                    else:
                        parts.append(conv_ref[9 * dz + 3 * dy + dx].astype(F32))
                bands.append(jnp.concatenate(parts, axis=1))
            for po in range(ZD):
                pieces = []
                for band in bands:
                    if po:
                        pieces.append(jnp.zeros((channels, po * channels), F32))
                    pieces.append(band)
                    rest = (ZD - 1 - po) * channels
                    if rest:
                        pieces.append(jnp.zeros((channels, rest), F32))
                row = (dy * ZD + po) * channels
                out_ref[row : row + channels] = jnp.concatenate(pieces, axis=1).astype(
                    BF16
                )


def toeplitz(conv_w):
    channels = conv_w.shape[1]
    shape = pltpu.VMEM((3 * ZD * channels, 3 * (ZD + 2) * channels), BF16)
    return pl.pallas_call(
        toeplitz_kernel,
        in_specs=[whole()],
        out_specs=[whole()] * 2,
        out_shape=[shape, shape],
        compiler_params=params(),
        name="toeplitz",
    )(conv_w)


def joined_planes(own, other, quarters):
    def blocks(pieces):
        return [
            ref[q]
            for ref, first, count in pieces
            for q in range(first * quarters, (first + count) * quarters)
        ]

    sums = [a.astype(F32) + b.astype(F32) for a, b in zip(blocks(own), blocks(other))]
    return [
        jnp.concatenate(sums[i : i + quarters], axis=1)
        for i in range(0, len(sums), quarters)
    ]


def store_shifted(out_ref, row, value):
    rows, cells = value.shape
    group = out_ref.shape[0] // 3
    wide = 2 * GX
    x = lax.rem(lax.broadcasted_iota(jnp.int32, (rows, wide), 1), GX)
    out_ref[group + row : group + row + rows] = value
    for first in range(0, cells, wide):
        cols = slice(first, first + wide)
        part = value[:, cols]
        out_ref[row : row + rows, cols] = jnp.where(
            x == 0, pltpu.roll(part, GX + 1, 1), pltpu.roll(part, 1, 1)
        )
        out_ref[2 * group + row : 2 * group + row + rows, cols] = jnp.where(
            x == GX - 1, pltpu.roll(part, GX - 1, 1), pltpu.roll(part, wide - 1, 1)
        )


def conv_planes(matrix_ref, shifted, partial, low_ref, high_ref):
    cells = shifted.shape[1]
    chunk = low_ref.shape[2]
    width = chunk // 2
    for first in range(0, cells, width):
        cols = slice(first, first + width)
        partial[:, cols] = jnp.dot(
            matrix_ref[...], shifted[:, cols], preferred_element_type=F32
        )
    channels = low_ref.shape[1]
    quarters = cells // chunk
    for po in range(ZD):
        rows = slice(po * channels, (po + 1) * channels)
        third = ZD * channels
        before = partial[rows, :]
        here = partial[third + po * channels : third + (po + 1) * channels, :]
        after = partial[2 * third + po * channels : 2 * third + (po + 1) * channels, :]
        result = (
            here + pltpu.roll(before, GX, 1) + pltpu.roll(after, cells - GX, 1)
        ).astype(BF16)
        out_ref = low_ref if po < ZH else high_ref
        first = (po % ZH) * quarters
        for q in range(quarters):
            out_ref[first + q] = result[:, q * chunk : (q + 1) * chunk]


def forward_kernel(
    down, middle, up, below, above, mix_ref, matrix_ref,
    low_ref, high_ref, plain_ref, shifted, partial,
):
    channels = mix_ref.shape[0]
    quarters = low_ref.shape[0] // ZH
    own = ((down, 1, ZH), (middle, 0, ZD - 2), (up, 0, ZH))
    other = ((below, 0, ZH + 1), (above, 0, ZH + 1))
    for p, plane in enumerate(joined_planes(own, other, quarters)):
        plane = plane.astype(BF16)
        plain_ref[p * channels : (p + 1) * channels] = plane
        mixed = jnp.dot(mix_ref[...], plane, preferred_element_type=F32)
        store_shifted(shifted, p * channels, mixed.astype(BF16))
    conv_planes(matrix_ref, shifted, partial, low_ref, high_ref)


def gradient_kernel(
    low, middle, high, below, above, plain_ref,
    keep_ref, send_ref, sums_ref, shifted, upstream,
):
    channels = low.shape[1]
    quarters = low.shape[0]
    cells = plain_ref.shape[1]
    for p in range(ZD + 2):
        rows = slice(p * channels, (p + 1) * channels)
        store_shifted(shifted, p * channels, plain_ref[rows])
    own = ((low, 0, 1), (middle, 0, ZD - 2), (high, 0, 1))
    planes = joined_planes(own, ((below, 0, ZH), (above, 0, ZH)), quarters)
    third = ZD * channels
    for p, plane in enumerate(planes):
        row = p * channels
        sums_ref[row : row + channels] = plane.astype(BF16)
        upstream[row : row + channels] = pltpu.roll(plane, cells - GX, 1).astype(BF16)
        upstream[third + row : third + row + channels] = plane.astype(BF16)
        upstream[2 * third + row : 2 * third + row + channels] = pltpu.roll(
            plane, GX, 1
        ).astype(BF16)
    wide = (ZD + 2) * channels
    blocks = []
    for dx in range(3):
        product = lax.dot_general(
            upstream[...],
            shifted[dx * wide : (dx + 1) * wide],
            (((1,), (1,)), ((), ())),
            preferred_element_type=F32,
        )
        for dy in range(3):
            block = None
            for po in range(ZD):
                row = (dy * ZD + po) * channels
                piece = product[
                    row : row + channels, po * channels : (po + 3) * channels
                ]
                block = piece if block is None else block + piece
            blocks.append(
                jnp.concatenate([block, jnp.zeros((channels, channels), F32)], axis=1)
            )
    half = keep_ref.shape[0]
    grads = jnp.concatenate(blocks, axis=0)
    first, second = grads[:half], grads[half:]
    odd = lax.rem(lax.axis_index("slab"), 2) == 1

    @pl.when(odd)
    def _():
        keep_ref[...] = second.astype(keep_ref.dtype)
        send_ref[...] = first.astype(send_ref.dtype)

    @pl.when(jnp.logical_not(odd))
    def _():
        keep_ref[...] = first.astype(keep_ref.dtype)
        send_ref[...] = second.astype(send_ref.dtype)


def backward_kernel(
    down, up, below, above, sums_ref, matrix_ref, low_ref, high_ref, shifted, partial
):
    channels = low_ref.shape[1]
    quarters = below.shape[0]
    (first,) = joined_planes(((down, 1, 1),), ((below, 0, 1),), quarters)
    (last,) = joined_planes(((up, 0, 1),), ((above, 0, 1),), quarters)
    store_shifted(shifted, 0, first.astype(BF16))
    for p in range(ZD):
        rows = slice(p * channels, (p + 1) * channels)
        store_shifted(shifted, (p + 1) * channels, sums_ref[rows])
    store_shifted(shifted, (ZD + 1) * channels, last.astype(BF16))
    conv_planes(matrix_ref, shifted, partial, low_ref, high_ref)


def gather_kernel(
    atom_hbm, cell_hbm, live_ref, weight_ref, mix_ref,
    a0, a1, a2, a3, b0, b1, b2, b3, potential_ref, grad_ref,
    atom_ref, cell_ref, small_sems, field, total,
):
    channels = mix_ref.shape[0]
    tiles, tile_a, tile_c = weight_ref.shape
    half = tile_c // 2
    small = copies(((atom_hbm, atom_ref), (cell_hbm, cell_ref)), small_sems)
    for copy in small:
        copy.start()
    first = 0
    for a, b in ((a0, b0), (a1, b1), (a2, b2), (a3, b3)):
        count = a.shape[0]
        for i, cols in enumerate((slice(0, half), slice(half, tile_c))):
            row = 2 * i * channels
            field[first : first + count, row : row + channels] = a[:, :, cols]
            field[first : first + count, row + channels : row + 2 * channels] = b[
                :, :, cols
            ]
        first += count
    total[...] = jnp.zeros_like(total)
    for copy in small:
        copy.wait()
    live = live_ref[0, 0]
    lane = lax.broadcasted_iota(jnp.int32, (2 * channels, 2 * tile_a), 1)
    for j in range(0, tiles, 2):
        pair = (j, j + 1)
        left = jnp.concatenate([field[cell_ref[0, t]] for t in pair], axis=0)
        right = jnp.concatenate(
            [
                weight_ref[t, :, cols]
                for t in pair
                for cols in (slice(0, half), slice(half, tile_c))
            ],
            axis=0,
        )
        product = lax.dot_general(
            left, right, (((1,), (1,)), ((), ())), preferred_element_type=F32
        )
        for i, t in enumerate(pair):
            row, col = 4 * i * channels, 2 * i * tile_a
            both = jnp.where(
                lane < tile_a,
                product[row : row + 2 * channels, col : col + 2 * tile_a],
                product[row + 2 * channels : row + 4 * channels, col : col + 2 * tile_a],
            )
            total[atom_ref[0, t]] += jnp.where(t < live, both, jnp.zeros_like(both))

    for a in range(0, total.shape[0], 2):
        lower, upper = total[a], total[a + 1]
        pair = jnp.where(
            lane < tile_a,
            lower + pltpu.roll(lower, tile_a, 1),
            upper + pltpu.roll(upper, tile_a, 1),
        ).astype(BF16)
        cols = slice(a * tile_a, (a + 2) * tile_a)
        potential_ref[:, cols] = pair[:channels]
        grad_ref[:, cols] = lax.dot_general(
            mix_ref[...], pair[channels:], (((0,), (0,)), ((), ())),
            preferred_element_type=F32,
        ).astype(BF16)


def gather(phi, drho, weights, atom_ids, cell_ids, live, w_mix, atoms):
    _, tile_a, tile_c = weights.shape
    channels = w_mix.shape[0]
    blocks = sum(part.shape[0] for part in phi)
    shape = jax.ShapeDtypeStruct((channels, atoms), BF16)
    return pl.pallas_call(
        gather_kernel,
        in_specs=list_specs() + [whole()] * 10,
        out_specs=[whole()] * 2,
        out_shape=[shape, shape],
        scratch_shapes=list_scratch(atom_ids, cell_ids)
        + [
            pltpu.VMEM((blocks, 4 * channels, tile_c // 2), BF16),
            pltpu.VMEM((atoms // tile_a, 2 * channels, 2 * tile_a), F32),
        ],
        compiler_params=params(),
        name="gather",
    )(*in_hbm(atom_ids, cell_ids), live, weights, w_mix, *phi, *drho)


def finish_kernel(
    mine_ref, other_ref, mix_ref, conv_ref, conv_out, mix_out,
    *, conv_scale, mix_scale,
):
    channels = mix_ref.shape[0]
    mine, other = mine_ref[...].astype(F32), other_ref[...].astype(F32)
    odd = lax.rem(lax.axis_index("slab"), 2) == 1
    total = jnp.concatenate(
        [jnp.where(odd, other, mine), jnp.where(odd, mine, other)], axis=0
    )
    mix = mix_ref[...]
    acc = jnp.zeros((channels, channels), F32)
    for dz in range(3):
        part = total[:, dz * channels : (dz + 1) * channels]
        upper = part.astype(BF16)
        pieces = (upper, (part - upper.astype(F32)).astype(BF16))
        kernels = jnp.concatenate(
            [conv_ref[9 * dz + 3 * (n % 3) + n // 3] for n in range(9)], axis=0
        )
        scaled = jnp.zeros(part.shape, F32)
        for piece in pieces:
            scaled = scaled + lax.dot_general(
                piece, mix, (((1,), (1,)), ((), ())), preferred_element_type=F32
            )
            acc = acc + lax.dot_general(
                kernels, piece, (((0,), (0,)), ((), ())), preferred_element_type=F32
            )
        scaled = scaled * (1.0 / conv_scale)
        for n in range(9):
            conv_out[9 * dz + 3 * (n % 3) + n // 3] = scaled[
                n * channels : (n + 1) * channels
            ]
    mix_out[...] = acc * (1.0 / mix_scale)


def ring(value, axis, steps):
    count = lax.axis_size(axis)
    pairs = [(source, (source + steps) % count) for source in range(count)]
    return pltpu.with_memory_space_constraint(
        lax.ppermute(value, axis, pairs), pltpu.VMEM
    )


def exchanged(value, axis, stride):
    count = lax.axis_size(axis)
    return lax.ppermute(value, axis, [(i, i ^ stride) for i in range(count)])


def local(feats, tile_weight, tile_atom, tile_cell, tile_live, w_mix, conv_w, cotangent):
    return step(
        feats[0], tile_weight[0], tile_atom, tile_cell, tile_live,
        w_mix, conv_w, cotangent[0],
    )


def step(feats, weights, atom_ids, cell_ids, live, w_mix, conv_w, cot):
    channels, atoms = feats.shape
    tile_c = weights.shape[2]
    quarters = GY * GX // tile_c
    cells = GY * GX
    smem = pl.BlockSpec(memory_space=pltpu.SMEM)

    dd, dm, du, held = first_deposit(feats, weights, atom_ids, cell_ids, live)
    d_below, d_above = ring(du, "slab", 1), ring(dd, "slab", -1)
    ed, el, em, eh, eu = second_deposit(cot, held, atom_ids, cell_ids, live)
    e_below, e_above = ring(eu, "slab", 1), ring(ed, "slab", -1)
    f_below, f_above = ring(eh, "slab", 1), ring(el, "slab", -1)
    forward, backward = toeplitz(conv_w)

    half = pltpu.VMEM((ZH * quarters, channels, tile_c), BF16)
    rows = (ZD + 2) * channels
    scratch = [
        pltpu.VMEM((3 * rows, cells), BF16),
        pltpu.VMEM((3 * ZD * channels, cells), F32),
    ]
    phi_low, phi_high, plain = pl.pallas_call(
        forward_kernel,
        in_specs=[whole()] * 7,
        out_specs=[whole()] * 3,
        out_shape=[half, half, pltpu.VMEM((rows, cells), BF16)],
        scratch_shapes=scratch,
        compiler_params=params(),
        name="forward",
    )(dd, dm, du, d_below, d_above, w_mix, forward)
    phi_below, phi_above = ring(phi_high, "slab", 1), ring(phi_low, "slab", -1)

    part = pltpu.VMEM((9 * channels // 2, 4 * channels), BF16)
    keep, send, sums = pl.pallas_call(
        gradient_kernel,
        in_specs=[whole()] * 6,
        out_specs=[whole()] * 3,
        out_shape=[pltpu.VMEM(part.shape, F32), part, pltpu.VMEM((ZD * channels, cells), BF16)],
        scratch_shapes=[scratch[0], pltpu.VMEM((3 * ZD * channels, cells), BF16)],
        compiler_params=params(),
        name="gradient",
    )(el, em, eh, e_below, e_above, plain)
    arrived = exchanged(send, "slab", 1)
    drho_low, drho_high = pl.pallas_call(
        backward_kernel,
        in_specs=[whole()] * 6,
        out_specs=[whole()] * 2,
        out_shape=[half, half],
        scratch_shapes=scratch,
        compiler_params=params(),
        name="backward",
    )(ed, eu, f_below, f_above, sums, backward)
    drho_below, drho_above = ring(drho_high, "slab", 1), ring(drho_low, "slab", -1)

    total = (keep + arrived.astype(F32)).astype(BF16)
    for turn in range((lax.axis_size("rep") - 1).bit_length()):
        arrived = exchanged(total, "rep", 1 << turn)
        total = total + arrived
    strides = [1 << i for i in range(1, (lax.axis_size("slab") - 1).bit_length())]
    for stride in strides[:-2]:
        arrived = exchanged(total, "slab", stride)
        total = total + arrived
    near, far = strides[-2:]
    across = [exchanged(total, "slab", s) for s in (near, far, near | far)]
    total = ((total + across[0]) + (across[1] + across[2])).astype(BF16)
    other = exchanged(total, "slab", 1)

    groups = lax.axis_size("rep") * lax.axis_size("slab")
    conv_grad, mix_grad = pl.pallas_call(
        functools.partial(
            finish_kernel,
            conv_scale=math.sqrt(groups * ZD * cells),
            mix_scale=math.sqrt(groups * atoms),
        ),
        in_specs=[whole()] * 4,
        out_specs=[whole()] * 2,
        out_shape=[
            jax.ShapeDtypeStruct(conv_w.shape, F32),
            jax.ShapeDtypeStruct(w_mix.shape, F32),
        ],
        compiler_params=params(),
        name="finish",
    )(total, other, w_mix, conv_w)

    potential, feats_grad = gather(
        (phi_below, phi_low, phi_high, phi_above),
        (drho_below, drho_low, drho_high, drho_above),
        weights, atom_ids, cell_ids, live, w_mix, atoms,
    )
    return potential[None], feats_grad[None], conv_grad, mix_grad


def solution(mesh):
    return jax.shard_map(
        local,
        mesh=mesh,
        in_specs=(
            P("rep", None, "slab"),
            P("rep", "slab", None, None),
            P("rep", "slab"),
            P("rep", "slab"),
            P("rep", "slab"),
            P(),
            P(),
            P("rep", None, "slab"),
        ),
        out_specs=(P("rep", None, "slab"), P("rep", None, "slab"), P(), P()),
        check_vma=False,
    )
```

```python
import functools
import math

import jax
import jax.numpy as jnp
from jax import lax
from jax.experimental import pallas as pl
from jax.experimental.pallas import tpu as pltpu
from jax.sharding import PartitionSpec as P

GY = 32
GX = 64
ZD = 4
ZH = 2
F32 = jnp.float32
BF16 = jnp.bfloat16
VMEM_LIMIT = 16 * 1024 * 1024


def params(*semantics):
    return pltpu.CompilerParams(
        dimension_semantics=semantics or None, vmem_limit_bytes=VMEM_LIMIT
    )


def whole():
    return pl.BlockSpec(memory_space=pltpu.VMEM)


def copies(pairs, sems):
    return [
        pltpu.make_async_copy(source, target, sems.at[i])
        for i, (source, target) in enumerate(pairs)
    ]


def add_tiles(tiles, atom_ref, cell_ref, live, source, weight_ref, total):
    for j in range(tiles.start, tiles.stop):
        picked = source[atom_ref[0, j]]
        picked = jnp.where(j < live, picked, jnp.zeros_like(picked))
        total[cell_ref[0, j]] += jnp.dot(
            picked, weight_ref[j], preferred_element_type=F32
        )


def split_atoms(field, source):
    tile_a = source.shape[2]
    for a in range(source.shape[0]):
        source[a] = field[:, a * tile_a : (a + 1) * tile_a]


def write_parts(total, refs):
    first = 0
    for ref in refs:
        count = ref.shape[0]
        ref[...] = total[first : first + count].astype(BF16)
        first += count


def first_deposit_kernel(
    atom_hbm, cell_hbm, live_ref, feats_hbm, weight_hbm,
    down_ref, middle_ref, up_ref, weight_ref,
    atom_ref, cell_ref, small_sems, source, total, feats, weight_sems,
):
    chunks = weight_sems.shape[0]
    per_chunk = weight_ref.shape[0] // chunks
    small = copies(
        ((atom_hbm, atom_ref), (cell_hbm, cell_ref), (feats_hbm, feats)), small_sems
    )
    parts = [slice(i * per_chunk, (i + 1) * per_chunk) for i in range(chunks)]
    large = copies([(weight_hbm.at[p], weight_ref.at[p]) for p in parts], weight_sems)
    ahead = chunks
    for copy in small + large[:ahead]:
        copy.start()
    total[...] = jnp.zeros_like(total)
    for copy in small:
        copy.wait()
    split_atoms(feats[...], source)
    live = live_ref[0, 0]
    for i, (part, copy) in enumerate(zip(parts, large)):
        copy.wait()
        if i + ahead < chunks:
            large[i + ahead].start()
        add_tiles(part, atom_ref, cell_ref, live, source, weight_ref, total)
    write_parts(total, (down_ref, middle_ref, up_ref))


def second_deposit_kernel(
    atom_hbm, cell_hbm, live_ref, cot_ref, weight_ref,
    *rest,
):
    *parts, atom_ref, cell_ref, small_sems, source, total = rest
    small = copies(((atom_hbm, atom_ref), (cell_hbm, cell_ref)), small_sems)
    for copy in small:
        copy.start()
    total[...] = jnp.zeros_like(total)
    split_atoms(cot_ref[...], source)
    for copy in small:
        copy.wait()
    tiles = slice(0, weight_ref.shape[0])
    add_tiles(tiles, atom_ref, cell_ref, live_ref[0, 0], source, weight_ref, total)
    write_parts(total, parts)


def in_hbm(*values):
    return [pltpu.with_memory_space_constraint(value, pltpu.HBM) for value in values]


def hbm():
    return pl.BlockSpec(memory_space=pltpu.HBM)


def list_scratch(atom_ids, cell_ids):
    return [
        pltpu.SMEM(atom_ids.shape, jnp.int32),
        pltpu.SMEM(cell_ids.shape, jnp.int32),
        pltpu.SemaphoreType.DMA((3,)),
    ]


def list_specs():
    return [hbm(), hbm(), pl.BlockSpec(memory_space=pltpu.SMEM)]


def deposit_shapes(field, weights, planes_of):
    channels, atoms = field.shape
    _, tile_a, tile_c = weights.shape
    quarters = GY * GX // tile_c
    parts = [
        pltpu.VMEM((planes * quarters, channels, tile_c), BF16)
        for planes in planes_of
    ]
    scratch = [
        pltpu.VMEM((atoms // tile_a, channels, tile_a), BF16),
        pltpu.VMEM(((ZD + 2 * ZH) * quarters, channels, tile_c), F32),
    ]
    return parts, scratch


def first_deposit(feats, weights, atom_ids, cell_ids, live):
    parts, scratch = deposit_shapes(feats, weights, (ZH + 1, ZD - 2, ZH + 1))
    return pl.pallas_call(
        first_deposit_kernel,
        in_specs=list_specs() + [hbm()] * 2,
        out_specs=[whole()] * 4,
        out_shape=parts + [pltpu.VMEM(weights.shape, BF16)],
        scratch_shapes=list_scratch(atom_ids, cell_ids)
        + scratch
        + [pltpu.VMEM(feats.shape, BF16), pltpu.SemaphoreType.DMA((2,))],
        compiler_params=params(),
        name="first_deposit",
    )(*in_hbm(atom_ids, cell_ids), live, *in_hbm(feats, weights))


def second_deposit(cot, weights, atom_ids, cell_ids, live):
    parts, scratch = deposit_shapes(cot, weights, (ZH, 1, ZD - 2, 1, ZH))
    return pl.pallas_call(
        second_deposit_kernel,
        in_specs=list_specs() + [whole()] * 2,
        out_specs=[whole()] * len(parts),
        out_shape=parts,
        scratch_shapes=list_scratch(atom_ids, cell_ids) + scratch,
        compiler_params=params(),
        name="second_deposit",
    )(*in_hbm(atom_ids, cell_ids), live, cot, weights)


def toeplitz_kernel(conv_ref, forward_ref, backward_ref):
    channels = conv_ref.shape[1]
    for flip, out_ref in ((False, forward_ref), (True, backward_ref)):
        for dy in range(3):
            bands = []
            for dx in range(3):
                parts = []
                for dz in range(3):
                    if flip:
                        k = 9 * (2 - dz) + 3 * (2 - dy) + (2 - dx)
                        parts.append(conv_ref[k].astype(F32).T)
                    else:
                        parts.append(conv_ref[9 * dz + 3 * dy + dx].astype(F32))
                bands.append(jnp.concatenate(parts, axis=1))
            for po in range(ZD):
                pieces = []
                for band in bands:
                    if po:
                        pieces.append(jnp.zeros((channels, po * channels), F32))
                    pieces.append(band)
                    rest = (ZD - 1 - po) * channels
                    if rest:
                        pieces.append(jnp.zeros((channels, rest), F32))
                row = (dy * ZD + po) * channels
                out_ref[row : row + channels] = jnp.concatenate(pieces, axis=1).astype(
                    BF16
                )


def toeplitz(conv_w):
    channels = conv_w.shape[1]
    shape = pltpu.VMEM((3 * ZD * channels, 3 * (ZD + 2) * channels), BF16)
    return pl.pallas_call(
        toeplitz_kernel,
        in_specs=[whole()],
        out_specs=[whole()] * 2,
        out_shape=[shape, shape],
        compiler_params=params(),
        name="toeplitz",
    )(conv_w)


def joined_planes(own, other, quarters):
    def blocks(pieces):
        return [
            ref[q]
            for ref, first, count in pieces
            for q in range(first * quarters, (first + count) * quarters)
        ]

    sums = [a.astype(F32) + b.astype(F32) for a, b in zip(blocks(own), blocks(other))]
    return [
        jnp.concatenate(sums[i : i + quarters], axis=1)
        for i in range(0, len(sums), quarters)
    ]


def store_shifted(out_ref, row, value):
    rows, cells = value.shape
    group = out_ref.shape[0] // 3
    wide = 2 * GX
    x = lax.rem(lax.broadcasted_iota(jnp.int32, (rows, wide), 1), GX)
    out_ref[group + row : group + row + rows] = value
    for first in range(0, cells, wide):
        cols = slice(first, first + wide)
        part = value[:, cols]
        out_ref[row : row + rows, cols] = jnp.where(
            x == 0, pltpu.roll(part, GX + 1, 1), pltpu.roll(part, 1, 1)
        )
        out_ref[2 * group + row : 2 * group + row + rows, cols] = jnp.where(
            x == GX - 1, pltpu.roll(part, GX - 1, 1), pltpu.roll(part, wide - 1, 1)
        )


def conv_planes(matrix_ref, shifted, partial, low_ref, high_ref):
    cells = shifted.shape[1]
    chunk = low_ref.shape[2]
    width = chunk // 2
    for first in range(0, cells, width):
        cols = slice(first, first + width)
        partial[:, cols] = jnp.dot(
            matrix_ref[...], shifted[:, cols], preferred_element_type=F32
        )
    channels = low_ref.shape[1]
    quarters = cells // chunk
    for po in range(ZD):
        rows = slice(po * channels, (po + 1) * channels)
        third = ZD * channels
        before = partial[rows, :]
        here = partial[third + po * channels : third + (po + 1) * channels, :]
        after = partial[2 * third + po * channels : 2 * third + (po + 1) * channels, :]
        result = (
            here + pltpu.roll(before, GX, 1) + pltpu.roll(after, cells - GX, 1)
        ).astype(BF16)
        out_ref = low_ref if po < ZH else high_ref
        first = (po % ZH) * quarters
        for q in range(quarters):
            out_ref[first + q] = result[:, q * chunk : (q + 1) * chunk]


def forward_kernel(
    down, middle, up, below, above, mix_ref, matrix_ref,
    low_ref, high_ref, plain_ref, shifted, partial,
):
    channels = mix_ref.shape[0]
    quarters = low_ref.shape[0] // ZH
    own = ((down, 1, ZH), (middle, 0, ZD - 2), (up, 0, ZH))
    other = ((below, 0, ZH + 1), (above, 0, ZH + 1))
    for p, plane in enumerate(joined_planes(own, other, quarters)):
        plane = plane.astype(BF16)
        store_shifted(plain_ref, p * channels, plane)
        mixed = jnp.dot(mix_ref[...], plane, preferred_element_type=F32)
        store_shifted(shifted, p * channels, mixed.astype(BF16))
    conv_planes(matrix_ref, shifted, partial, low_ref, high_ref)


def gradient_kernel(
    low, middle, high, below, above, shifted,
    keep_ref, send_ref, sums_ref, upstream,
):
    channels = low.shape[1]
    quarters = low.shape[0]
    cells = shifted.shape[1]
    own = ((low, 0, 1), (middle, 0, ZD - 2), (high, 0, 1))
    planes = joined_planes(own, ((below, 0, ZH), (above, 0, ZH)), quarters)
    third = ZD * channels
    for p, plane in enumerate(planes):
        row = p * channels
        plane = plane.astype(BF16)
        sums_ref[row : row + channels] = plane
        upstream[row : row + channels] = pltpu.roll(plane, cells - GX, 1)
        upstream[third + row : third + row + channels] = plane
        upstream[2 * third + row : 2 * third + row + channels] = pltpu.roll(plane, GX, 1)
    wide = (ZD + 2) * channels
    blocks = []
    for dx in range(3):
        product = lax.dot_general(
            upstream[...],
            shifted[dx * wide : (dx + 1) * wide],
            (((1,), (1,)), ((), ())),
            preferred_element_type=F32,
        )
        for dy in range(3):
            block = None
            for po in range(ZD):
                row = (dy * ZD + po) * channels
                piece = product[
                    row : row + channels, po * channels : (po + 3) * channels
                ]
                block = piece if block is None else block + piece
            blocks.append(
                jnp.concatenate([block, jnp.zeros((channels, channels), F32)], axis=1)
            )
    half = keep_ref.shape[0]
    grads = jnp.concatenate(blocks, axis=0)
    first, second = grads[:half], grads[half:]
    odd = lax.rem(lax.axis_index("slab"), 2) == 1

    @pl.when(odd)
    def _():
        keep_ref[...] = second.astype(keep_ref.dtype)
        send_ref[...] = first.astype(send_ref.dtype)

    @pl.when(jnp.logical_not(odd))
    def _():
        keep_ref[...] = first.astype(keep_ref.dtype)
        send_ref[...] = second.astype(send_ref.dtype)


def backward_kernel(
    down, up, below, above, sums_ref, matrix_ref, low_ref, high_ref, shifted, partial
):
    channels = low_ref.shape[1]
    quarters = below.shape[0]
    (first,) = joined_planes(((down, 1, 1),), ((below, 0, 1),), quarters)
    (last,) = joined_planes(((up, 0, 1),), ((above, 0, 1),), quarters)
    store_shifted(shifted, 0, first.astype(BF16))
    for p in range(ZD):
        rows = slice(p * channels, (p + 1) * channels)
        store_shifted(shifted, (p + 1) * channels, sums_ref[rows])
    store_shifted(shifted, (ZD + 1) * channels, last.astype(BF16))
    conv_planes(matrix_ref, shifted, partial, low_ref, high_ref)


def gather_kernel(
    atom_ref, cell_ref, live_ref, weight_ref, mix_ref,
    a0, a1, a2, a3, b0, b1, b2, b3, potential_ref, grad_ref, field, total,
):
    channels = mix_ref.shape[0]
    tiles, tile_a, tile_c = weight_ref.shape
    half = tile_c // 2
    first = 0
    for a, b in ((a0, b0), (a1, b1), (a2, b2), (a3, b3)):
        count = a.shape[0]
        for i, cols in enumerate((slice(0, half), slice(half, tile_c))):
            row = 2 * i * channels
            field[first : first + count, row : row + channels] = a[:, :, cols]
            field[first : first + count, row + channels : row + 2 * channels] = b[
                :, :, cols
            ]
        first += count
    total[...] = jnp.zeros_like(total)
    live = live_ref[0, 0]
    lane = lax.broadcasted_iota(jnp.int32, (2 * channels, 2 * tile_a), 1)
    for j in range(0, tiles, 2):
        pair = (j, j + 1)
        left = jnp.concatenate([field[cell_ref[0, t]] for t in pair], axis=0)
        right = jnp.concatenate(
            [
                weight_ref[t, :, cols]
                for t in pair
                for cols in (slice(0, half), slice(half, tile_c))
            ],
            axis=0,
        )
        product = lax.dot_general(
            left, right, (((1,), (1,)), ((), ())), preferred_element_type=F32
        )
        for i, t in enumerate(pair):
            row, col = 4 * i * channels, 2 * i * tile_a
            both = jnp.where(
                lane < tile_a,
                product[row : row + 2 * channels, col : col + 2 * tile_a],
                product[row + 2 * channels : row + 4 * channels, col : col + 2 * tile_a],
            )
            total[atom_ref[0, t]] += jnp.where(t < live, both, jnp.zeros_like(both))

    for a in range(0, total.shape[0], 2):
        lower, upper = total[a], total[a + 1]
        pair = jnp.where(
            lane < tile_a,
            lower + pltpu.roll(lower, tile_a, 1),
            upper + pltpu.roll(upper, tile_a, 1),
        ).astype(BF16)
        cols = slice(a * tile_a, (a + 2) * tile_a)
        potential_ref[:, cols] = pair[:channels]
        grad_ref[:, cols] = lax.dot_general(
            mix_ref[...], pair[channels:], (((0,), (0,)), ((), ())),
            preferred_element_type=F32,
        ).astype(BF16)


def gather(phi, drho, weights, atom_ids, cell_ids, live, w_mix, atoms):
    _, tile_a, tile_c = weights.shape
    channels = w_mix.shape[0]
    blocks = sum(part.shape[0] for part in phi)
    shape = jax.ShapeDtypeStruct((channels, atoms), BF16)
    return pl.pallas_call(
        gather_kernel,
        in_specs=[pl.BlockSpec(memory_space=pltpu.SMEM)] * 3 + [whole()] * 10,
        out_specs=[whole()] * 2,
        out_shape=[shape, shape],
        scratch_shapes=[
            pltpu.VMEM((blocks, 4 * channels, tile_c // 2), BF16),
            pltpu.VMEM((atoms // tile_a, 2 * channels, 2 * tile_a), F32),
        ],
        compiler_params=params(),
        name="gather",
    )(atom_ids, cell_ids, live, weights, w_mix, *phi, *drho)


def finish_kernel(
    mine_ref, other_ref, mix_ref, conv_ref, conv_out, mix_out,
    *, conv_scale, mix_scale,
):
    channels = mix_ref.shape[0]
    mine, other = mine_ref[...].astype(F32), other_ref[...].astype(F32)
    odd = lax.rem(lax.axis_index("slab"), 2) == 1
    total = jnp.concatenate(
        [jnp.where(odd, other, mine), jnp.where(odd, mine, other)], axis=0
    )
    mix = mix_ref[...]
    acc = jnp.zeros((channels, channels), F32)
    for dz in range(3):
        part = total[:, dz * channels : (dz + 1) * channels]
        upper = part.astype(BF16)
        pieces = (upper, (part - upper.astype(F32)).astype(BF16))
        kernels = jnp.concatenate(
            [conv_ref[9 * dz + 3 * (n % 3) + n // 3] for n in range(9)], axis=0
        )
        scaled = jnp.zeros(part.shape, F32)
        for piece in pieces:
            scaled = scaled + lax.dot_general(
                piece, mix, (((1,), (1,)), ((), ())), preferred_element_type=F32
            )
            acc = acc + lax.dot_general(
                kernels, piece, (((0,), (0,)), ((), ())), preferred_element_type=F32
            )
        scaled = scaled * (1.0 / conv_scale)
        for n in range(9):
            conv_out[9 * dz + 3 * (n % 3) + n // 3] = scaled[
                n * channels : (n + 1) * channels
            ]
    mix_out[...] = acc * (1.0 / mix_scale)


def ring(value, axis, steps):
    count = lax.axis_size(axis)
    pairs = [(source, (source + steps) % count) for source in range(count)]
    return pltpu.with_memory_space_constraint(
        lax.ppermute(value, axis, pairs), pltpu.VMEM
    )


def exchanged(value, axis, stride):
    count = lax.axis_size(axis)
    return lax.ppermute(value, axis, [(i, i ^ stride) for i in range(count)])


def local(feats, tile_weight, tile_atom, tile_cell, tile_live, w_mix, conv_w, cotangent):
    return step(
        feats[0], tile_weight[0], tile_atom, tile_cell, tile_live,
        w_mix, conv_w, cotangent[0],
    )


def step(feats, weights, atom_ids, cell_ids, live, w_mix, conv_w, cot):
    channels, atoms = feats.shape
    tile_c = weights.shape[2]
    quarters = GY * GX // tile_c
    cells = GY * GX
    smem = pl.BlockSpec(memory_space=pltpu.SMEM)

    dd, dm, du, held = first_deposit(feats, weights, atom_ids, cell_ids, live)
    d_below, d_above = ring(du, "slab", 1), ring(dd, "slab", -1)
    ed, el, em, eh, eu = second_deposit(cot, held, atom_ids, cell_ids, live)
    e_below, e_above = ring(eu, "slab", 1), ring(ed, "slab", -1)
    f_below, f_above = ring(eh, "slab", 1), ring(el, "slab", -1)
    forward, backward = toeplitz(conv_w)

    half = pltpu.VMEM((ZH * quarters, channels, tile_c), BF16)
    rows = (ZD + 2) * channels
    scratch = [
        pltpu.VMEM((3 * rows, cells), BF16),
        pltpu.VMEM((3 * ZD * channels, cells), F32),
    ]
    phi_low, phi_high, plain = pl.pallas_call(
        forward_kernel,
        in_specs=[whole()] * 7,
        out_specs=[whole()] * 3,
        out_shape=[half, half, pltpu.VMEM((3 * rows, cells), BF16)],
        scratch_shapes=scratch,
        compiler_params=params(),
        name="forward",
    )(dd, dm, du, d_below, d_above, w_mix, forward)
    phi_below, phi_above = ring(phi_high, "slab", 1), ring(phi_low, "slab", -1)

    part = pltpu.VMEM((9 * channels // 2, 4 * channels), BF16)
    keep, send, sums = pl.pallas_call(
        gradient_kernel,
        in_specs=[whole()] * 6,
        out_specs=[whole()] * 3,
        out_shape=[pltpu.VMEM(part.shape, F32), part, pltpu.VMEM((ZD * channels, cells), BF16)],
        scratch_shapes=[pltpu.VMEM((3 * ZD * channels, cells), BF16)],
        compiler_params=params(),
        name="gradient",
    )(el, em, eh, e_below, e_above, plain)
    arrived = exchanged(send, "slab", 1)
    drho_low, drho_high = pl.pallas_call(
        backward_kernel,
        in_specs=[whole()] * 6,
        out_specs=[whole()] * 2,
        out_shape=[half, half],
        scratch_shapes=scratch,
        compiler_params=params(),
        name="backward",
    )(ed, eu, f_below, f_above, sums, backward)
    drho_below, drho_above = ring(drho_high, "slab", 1), ring(drho_low, "slab", -1)

    total = (keep + arrived.astype(F32)).astype(BF16)
    for turn in range((lax.axis_size("rep") - 1).bit_length()):
        arrived = exchanged(total, "rep", 1 << turn)
        total = total + arrived
    strides = [1 << i for i in range(1, (lax.axis_size("slab") - 1).bit_length())]
    for stride in strides[:-2]:
        arrived = exchanged(total, "slab", stride)
        total = total + arrived
    near, far = strides[-2:]
    across = [exchanged(total, "slab", s) for s in (near, far, near | far)]
    total = ((total + across[0]) + (across[1] + across[2])).astype(BF16)
    other = exchanged(total, "slab", 1)

    groups = lax.axis_size("rep") * lax.axis_size("slab")
    conv_grad, mix_grad = pl.pallas_call(
        functools.partial(
            finish_kernel,
            conv_scale=math.sqrt(groups * ZD * cells),
            mix_scale=math.sqrt(groups * atoms),
        ),
        in_specs=[whole()] * 4,
        out_specs=[whole()] * 2,
        out_shape=[
            jax.ShapeDtypeStruct(conv_w.shape, F32),
            jax.ShapeDtypeStruct(w_mix.shape, F32),
        ],
        compiler_params=params(),
        name="finish",
    )(total, other, w_mix, conv_w)

    potential, feats_grad = gather(
        (phi_below, phi_low, phi_high, phi_above),
        (drho_below, drho_low, drho_high, drho_above),
        held, atom_ids, cell_ids, live, w_mix, atoms,
    )
    return potential[None], feats_grad[None], conv_grad, mix_grad


def solution(mesh):
    return jax.shard_map(
        local,
        mesh=mesh,
        in_specs=(
            P("rep", None, "slab"),
            P("rep", "slab", None, None),
            P("rep", "slab"),
            P("rep", "slab"),
            P("rep", "slab"),
            P(),
            P(),
            P("rep", None, "slab"),
        ),
        out_specs=(P("rep", None, "slab"), P("rep", None, "slab"), P(), P()),
        check_vma=False,
    )
```

```python
import functools
import math

import jax
import jax.numpy as jnp
from jax import lax
from jax.experimental import pallas as pl
from jax.experimental.pallas import tpu as pltpu
from jax.sharding import PartitionSpec as P

GY = 32
GX = 64
ZD = 4
ZH = 2
F32 = jnp.float32
BF16 = jnp.bfloat16
VMEM_LIMIT = 16 * 1024 * 1024


def params(*semantics):
    return pltpu.CompilerParams(
        dimension_semantics=semantics or None, vmem_limit_bytes=VMEM_LIMIT
    )


def whole():
    return pl.BlockSpec(memory_space=pltpu.VMEM)


def copies(pairs, sems):
    return [
        pltpu.make_async_copy(source, target, sems.at[i])
        for i, (source, target) in enumerate(pairs)
    ]


def add_tiles(tiles, atom_ref, cell_ref, live, source, weight_ref, total):
    for j in range(tiles.start, tiles.stop):
        picked = source[atom_ref[0, j]]
        picked = jnp.where(j < live, picked, jnp.zeros_like(picked))
        total[cell_ref[0, j]] += jnp.dot(
            picked, weight_ref[j], preferred_element_type=F32
        )


def split_atoms(field, source):
    tile_a = source.shape[2]
    for a in range(source.shape[0]):
        source[a] = field[:, a * tile_a : (a + 1) * tile_a]


def write_parts(total, refs):
    first = 0
    for ref in refs:
        count = ref.shape[0]
        ref[...] = total[first : first + count].astype(BF16)
        first += count


def first_deposit_kernel(
    atom_hbm, cell_hbm, live_ref, feats_hbm, weight_hbm,
    down_ref, middle_ref, up_ref, weight_ref,
    atom_ref, cell_ref, small_sems, source, total, feats, weight_sems,
):
    chunks = weight_sems.shape[0]
    per_chunk = weight_ref.shape[0] // chunks
    small = copies(
        ((atom_hbm, atom_ref), (cell_hbm, cell_ref), (feats_hbm, feats)), small_sems
    )
    parts = [slice(i * per_chunk, (i + 1) * per_chunk) for i in range(chunks)]
    large = copies([(weight_hbm.at[p], weight_ref.at[p]) for p in parts], weight_sems)
    ahead = chunks
    for copy in small + large[:ahead]:
        copy.start()
    total[...] = jnp.zeros_like(total)
    for copy in small:
        copy.wait()
    split_atoms(feats[...], source)
    live = live_ref[0, 0]
    for i, (part, copy) in enumerate(zip(parts, large)):
        copy.wait()
        if i + ahead < chunks:
            large[i + ahead].start()
        add_tiles(part, atom_ref, cell_ref, live, source, weight_ref, total)
    write_parts(total, (down_ref, middle_ref, up_ref))


def second_deposit_kernel(
    atom_hbm, cell_hbm, live_ref, cot_ref, weight_ref,
    *rest,
):
    *parts, atom_ref, cell_ref, small_sems, source, total = rest
    small = copies(((atom_hbm, atom_ref), (cell_hbm, cell_ref)), small_sems)
    for copy in small:
        copy.start()
    total[...] = jnp.zeros_like(total)
    split_atoms(cot_ref[...], source)
    for copy in small:
        copy.wait()
    tiles = slice(0, weight_ref.shape[0])
    add_tiles(tiles, atom_ref, cell_ref, live_ref[0, 0], source, weight_ref, total)
    write_parts(total, parts)


def in_hbm(*values):
    return [pltpu.with_memory_space_constraint(value, pltpu.HBM) for value in values]


def hbm():
    return pl.BlockSpec(memory_space=pltpu.HBM)


def list_scratch(atom_ids, cell_ids):
    return [
        pltpu.SMEM(atom_ids.shape, jnp.int32),
        pltpu.SMEM(cell_ids.shape, jnp.int32),
        pltpu.SemaphoreType.DMA((3,)),
    ]


def list_specs():
    return [hbm(), hbm(), pl.BlockSpec(memory_space=pltpu.SMEM)]


def deposit_shapes(field, weights, planes_of):
    channels, atoms = field.shape
    _, tile_a, tile_c = weights.shape
    quarters = GY * GX // tile_c
    parts = [
        pltpu.VMEM((planes * quarters, channels, tile_c), BF16)
        for planes in planes_of
    ]
    scratch = [
        pltpu.VMEM((atoms // tile_a, channels, tile_a), BF16),
        pltpu.VMEM(((ZD + 2 * ZH) * quarters, channels, tile_c), F32),
    ]
    return parts, scratch


def first_deposit(feats, weights, atom_ids, cell_ids, live):
    parts, scratch = deposit_shapes(feats, weights, (ZH + 1, ZD - 2, ZH + 1))
    return pl.pallas_call(
        first_deposit_kernel,
        in_specs=list_specs() + [hbm()] * 2,
        out_specs=[whole()] * 4,
        out_shape=parts + [pltpu.VMEM(weights.shape, BF16)],
        scratch_shapes=list_scratch(atom_ids, cell_ids)
        + scratch
        + [pltpu.VMEM(feats.shape, BF16), pltpu.SemaphoreType.DMA((2,))],
        compiler_params=params(),
        name="first_deposit",
    )(*in_hbm(atom_ids, cell_ids), live, *in_hbm(feats, weights))


def second_deposit(cot, weights, atom_ids, cell_ids, live):
    parts, scratch = deposit_shapes(cot, weights, (ZH, 1, ZD - 2, 1, ZH))
    return pl.pallas_call(
        second_deposit_kernel,
        in_specs=list_specs() + [whole()] * 2,
        out_specs=[whole()] * len(parts),
        out_shape=parts,
        scratch_shapes=list_scratch(atom_ids, cell_ids) + scratch,
        compiler_params=params(),
        name="second_deposit",
    )(*in_hbm(atom_ids, cell_ids), live, cot, weights)


def toeplitz_kernel(conv_ref, forward_ref, backward_ref):
    channels = conv_ref.shape[1]
    for flip, out_ref in ((False, forward_ref), (True, backward_ref)):
        for dy in range(3):
            bands = []
            for dx in range(3):
                parts = []
                for dz in range(3):
                    if flip:
                        k = 9 * (2 - dz) + 3 * (2 - dy) + (2 - dx)
                        parts.append(conv_ref[k].astype(F32).T)
                    else:
                        parts.append(conv_ref[9 * dz + 3 * dy + dx].astype(F32))
                bands.append(jnp.concatenate(parts, axis=1))
            for po in range(ZD):
                pieces = []
                for band in bands:
                    if po:
                        pieces.append(jnp.zeros((channels, po * channels), F32))
                    pieces.append(band)
                    rest = (ZD - 1 - po) * channels
                    if rest:
                        pieces.append(jnp.zeros((channels, rest), F32))
                row = (dy * ZD + po) * channels
                out_ref[row : row + channels] = jnp.concatenate(pieces, axis=1).astype(
                    BF16
                )


def toeplitz(conv_w):
    channels = conv_w.shape[1]
    shape = pltpu.VMEM((3 * ZD * channels, 3 * (ZD + 2) * channels), BF16)
    return pl.pallas_call(
        toeplitz_kernel,
        in_specs=[whole()],
        out_specs=[whole()] * 2,
        out_shape=[shape, shape],
        compiler_params=params(),
        name="toeplitz",
    )(conv_w)


def joined_planes(own, other, quarters):
    def blocks(pieces):
        return [
            ref[q]
            for ref, first, count in pieces
            for q in range(first * quarters, (first + count) * quarters)
        ]

    sums = [a.astype(F32) + b.astype(F32) for a, b in zip(blocks(own), blocks(other))]
    return [
        jnp.concatenate(sums[i : i + quarters], axis=1)
        for i in range(0, len(sums), quarters)
    ]


def store_shifted(out_ref, row, value):
    rows, cells = value.shape
    group = out_ref.shape[0] // 3
    wide = 2 * GX
    x = lax.rem(lax.broadcasted_iota(jnp.int32, (rows, wide), 1), GX)
    out_ref[group + row : group + row + rows] = value
    for first in range(0, cells, wide):
        cols = slice(first, first + wide)
        part = value[:, cols]
        out_ref[row : row + rows, cols] = jnp.where(
            x == 0, pltpu.roll(part, GX + 1, 1), pltpu.roll(part, 1, 1)
        )
        out_ref[2 * group + row : 2 * group + row + rows, cols] = jnp.where(
            x == GX - 1, pltpu.roll(part, GX - 1, 1), pltpu.roll(part, wide - 1, 1)
        )


def conv_planes(matrix_ref, shifted, partial, low_ref, high_ref):
    cells = shifted.shape[1]
    chunk = low_ref.shape[2]
    width = chunk // 2
    for first in range(0, cells, width):
        cols = slice(first, first + width)
        partial[:, cols] = jnp.dot(
            matrix_ref[...], shifted[:, cols], preferred_element_type=F32
        )
    channels = low_ref.shape[1]
    quarters = cells // chunk
    for po in range(ZD):
        rows = slice(po * channels, (po + 1) * channels)
        third = ZD * channels
        before = partial[rows, :]
        here = partial[third + po * channels : third + (po + 1) * channels, :]
        after = partial[2 * third + po * channels : 2 * third + (po + 1) * channels, :]
        result = (
            here + pltpu.roll(before, GX, 1) + pltpu.roll(after, cells - GX, 1)
        ).astype(BF16)
        out_ref = low_ref if po < ZH else high_ref
        first = (po % ZH) * quarters
        for q in range(quarters):
            out_ref[first + q] = result[:, q * chunk : (q + 1) * chunk]


def forward_kernel(
    down, middle, up, below, above, mix_ref, matrix_ref,
    low_ref, high_ref, plain_ref, shifted, partial,
):
    channels = mix_ref.shape[0]
    quarters = low_ref.shape[0] // ZH
    own = ((down, 1, ZH), (middle, 0, ZD - 2), (up, 0, ZH))
    other = ((below, 0, ZH + 1), (above, 0, ZH + 1))
    for p, plane in enumerate(joined_planes(own, other, quarters)):
        plane = plane.astype(BF16)
        store_shifted(plain_ref, p * channels, plane)
        mixed = jnp.dot(mix_ref[...], plane, preferred_element_type=F32)
        store_shifted(shifted, p * channels, mixed.astype(BF16))
    conv_planes(matrix_ref, shifted, partial, low_ref, high_ref)


def gradient_kernel(
    low, middle, high, below, above, shifted,
    keep_ref, send_ref, sums_ref, upstream,
):
    channels = low.shape[1]
    quarters = low.shape[0]
    cells = shifted.shape[1]
    own = ((low, 0, 1), (middle, 0, ZD - 2), (high, 0, 1))
    planes = joined_planes(own, ((below, 0, ZH), (above, 0, ZH)), quarters)
    third = ZD * channels
    for p, plane in enumerate(planes):
        row = p * channels
        plane = plane.astype(BF16)
        sums_ref[row : row + channels] = plane
        upstream[row : row + channels] = pltpu.roll(plane, cells - GX, 1)
        upstream[third + row : third + row + channels] = plane
        upstream[2 * third + row : 2 * third + row + channels] = pltpu.roll(plane, GX, 1)
    wide = (ZD + 2) * channels
    blocks = []
    for dx in range(3):
        product = lax.dot_general(
            upstream[...],
            shifted[dx * wide : (dx + 1) * wide],
            (((1,), (1,)), ((), ())),
            preferred_element_type=F32,
        )
        for dy in range(3):
            block = None
            for po in range(ZD):
                row = (dy * ZD + po) * channels
                piece = product[
                    row : row + channels, po * channels : (po + 3) * channels
                ]
                block = piece if block is None else block + piece
            blocks.append(
                jnp.concatenate([block, jnp.zeros((channels, channels), F32)], axis=1)
            )
    half = keep_ref.shape[0]
    grads = jnp.concatenate(blocks, axis=0)
    first, second = grads[:half], grads[half:]
    odd = lax.rem(lax.axis_index("slab"), 2) == 1

    @pl.when(odd)
    def _():
        keep_ref[...] = second.astype(keep_ref.dtype)
        send_ref[...] = first.astype(send_ref.dtype)

    @pl.when(jnp.logical_not(odd))
    def _():
        keep_ref[...] = first.astype(keep_ref.dtype)
        send_ref[...] = second.astype(send_ref.dtype)


def backward_kernel(
    down, up, below, above, sums_ref, matrix_ref, low_ref, high_ref, shifted, partial
):
    channels = low_ref.shape[1]
    quarters = below.shape[0]
    (first,) = joined_planes(((down, 1, 1),), ((below, 0, 1),), quarters)
    (last,) = joined_planes(((up, 0, 1),), ((above, 0, 1),), quarters)
    store_shifted(shifted, 0, first.astype(BF16))
    for p in range(ZD):
        rows = slice(p * channels, (p + 1) * channels)
        store_shifted(shifted, (p + 1) * channels, sums_ref[rows])
    store_shifted(shifted, (ZD + 1) * channels, last.astype(BF16))
    conv_planes(matrix_ref, shifted, partial, low_ref, high_ref)


def gather_kernel(
    atom_ref, cell_ref, live_ref, weight_ref, mix_ref,
    a0, a1, a2, a3, b0, b1, b2, b3, potential_ref, grad_ref, field, total,
):
    channels = mix_ref.shape[0]
    tiles, tile_a, tile_c = weight_ref.shape
    half = tile_c // 2
    first = 0
    for a, b in ((a0, b0), (a1, b1), (a2, b2), (a3, b3)):
        count = a.shape[0]
        for i, cols in enumerate((slice(0, half), slice(half, tile_c))):
            row = 2 * i * channels
            field[first : first + count, row : row + channels] = a[:, :, cols]
            field[first : first + count, row + channels : row + 2 * channels] = b[
                :, :, cols
            ]
        first += count
    total[...] = jnp.zeros_like(total)
    live = live_ref[0, 0]
    lane = lax.broadcasted_iota(jnp.int32, (2 * channels, 2 * tile_a), 1)
    for j in range(0, tiles, 2):
        pair = (j, j + 1)
        left = jnp.concatenate([field[cell_ref[0, t]] for t in pair], axis=0)
        right = jnp.concatenate(
            [
                weight_ref[t, :, cols]
                for t in pair
                for cols in (slice(0, half), slice(half, tile_c))
            ],
            axis=0,
        )
        product = lax.dot_general(
            left, right, (((1,), (1,)), ((), ())), preferred_element_type=F32
        )
        for i, t in enumerate(pair):
            row, col = 4 * i * channels, 2 * i * tile_a
            both = jnp.where(
                lane < tile_a,
                product[row : row + 2 * channels, col : col + 2 * tile_a],
                product[row + 2 * channels : row + 4 * channels, col : col + 2 * tile_a],
            )
            total[atom_ref[0, t]] += jnp.where(t < live, both, jnp.zeros_like(both))

    for a in range(0, total.shape[0], 2):
        lower, upper = total[a], total[a + 1]
        pair = jnp.where(
            lane < tile_a,
            lower + pltpu.roll(lower, tile_a, 1),
            upper + pltpu.roll(upper, tile_a, 1),
        ).astype(BF16)
        cols = slice(a * tile_a, (a + 2) * tile_a)
        potential_ref[:, cols] = pair[:channels]
        grad_ref[:, cols] = lax.dot_general(
            mix_ref[...], pair[channels:], (((0,), (0,)), ((), ())),
            preferred_element_type=F32,
        ).astype(BF16)


def gather(phi, drho, weights, atom_ids, cell_ids, live, w_mix, atoms):
    _, tile_a, tile_c = weights.shape
    channels = w_mix.shape[0]
    blocks = sum(part.shape[0] for part in phi)
    shape = jax.ShapeDtypeStruct((channels, atoms), BF16)
    return pl.pallas_call(
        gather_kernel,
        in_specs=[pl.BlockSpec(memory_space=pltpu.SMEM)] * 3 + [whole()] * 10,
        out_specs=[whole()] * 2,
        out_shape=[shape, shape],
        scratch_shapes=[
            pltpu.VMEM((blocks, 4 * channels, tile_c // 2), BF16),
            pltpu.VMEM((atoms // tile_a, 2 * channels, 2 * tile_a), F32),
        ],
        compiler_params=params(),
        name="gather",
    )(atom_ids, cell_ids, live, weights, w_mix, *phi, *drho)


def finish_kernel(
    mine_ref, other_ref, mix_ref, conv_ref, conv_out, mix_out,
    *, conv_scale, mix_scale,
):
    channels = mix_ref.shape[0]
    mine, other = mine_ref[...].astype(F32), other_ref[...].astype(F32)
    odd = lax.rem(lax.axis_index("slab"), 2) == 1
    total = jnp.concatenate(
        [jnp.where(odd, other, mine), jnp.where(odd, mine, other)], axis=0
    )
    mix = mix_ref[...]
    acc = jnp.zeros((channels, channels), F32)
    for dz in range(3):
        part = total[:, dz * channels : (dz + 1) * channels]
        upper = part.astype(BF16)
        pieces = (upper, (part - upper.astype(F32)).astype(BF16))
        kernels = jnp.concatenate(
            [conv_ref[9 * dz + 3 * (n % 3) + n // 3] for n in range(9)], axis=0
        )
        scaled = jnp.zeros(part.shape, F32)
        for piece in pieces:
            scaled = scaled + lax.dot_general(
                piece, mix, (((1,), (1,)), ((), ())), preferred_element_type=F32
            )
            acc = acc + lax.dot_general(
                kernels, piece, (((0,), (0,)), ((), ())), preferred_element_type=F32
            )
        scaled = scaled * (1.0 / conv_scale)
        for n in range(9):
            conv_out[9 * dz + 3 * (n % 3) + n // 3] = scaled[
                n * channels : (n + 1) * channels
            ]
    mix_out[...] = acc * (1.0 / mix_scale)


def ring(value, axis, steps):
    count = lax.axis_size(axis)
    pairs = [(source, (source + steps) % count) for source in range(count)]
    return pltpu.with_memory_space_constraint(
        lax.ppermute(value, axis, pairs), pltpu.VMEM
    )


def exchanged(value, axis, stride):
    count = lax.axis_size(axis)
    return lax.ppermute(value, axis, [(i, i ^ stride) for i in range(count)])


def local(feats, tile_weight, tile_atom, tile_cell, tile_live, w_mix, conv_w, cotangent):
    return step(
        feats[0], tile_weight[0], tile_atom, tile_cell, tile_live,
        w_mix, conv_w, cotangent[0],
    )


def step(feats, weights, atom_ids, cell_ids, live, w_mix, conv_w, cot):
    channels, atoms = feats.shape
    tile_c = weights.shape[2]
    quarters = GY * GX // tile_c
    cells = GY * GX
    smem = pl.BlockSpec(memory_space=pltpu.SMEM)

    dd, dm, du, held = first_deposit(feats, weights, atom_ids, cell_ids, live)
    d_below, d_above = ring(du, "slab", 1), ring(dd, "slab", -1)
    ed, el, em, eh, eu = second_deposit(cot, held, atom_ids, cell_ids, live)
    e_below, e_above = ring(eu, "slab", 1), ring(ed, "slab", -1)
    f_below, f_above = ring(eh, "slab", 1), ring(el, "slab", -1)
    forward, backward = toeplitz(conv_w)

    half = pltpu.VMEM((ZH * quarters, channels, tile_c), BF16)
    rows = (ZD + 2) * channels
    scratch = [
        pltpu.VMEM((3 * rows, cells), BF16),
        pltpu.VMEM((3 * ZD * channels, cells), F32),
    ]
    phi_low, phi_high, plain = pl.pallas_call(
        forward_kernel,
        in_specs=[whole()] * 7,
        out_specs=[whole()] * 3,
        out_shape=[half, half, pltpu.VMEM((3 * rows, cells), BF16)],
        scratch_shapes=scratch,
        compiler_params=params(),
        name="forward",
    )(dd, dm, du, d_below, d_above, w_mix, forward)
    phi_below, phi_above = ring(phi_high, "slab", 1), ring(phi_low, "slab", -1)

    part = pltpu.VMEM((9 * channels // 2, 4 * channels), BF16)
    keep, send, sums = pl.pallas_call(
        gradient_kernel,
        in_specs=[whole()] * 6,
        out_specs=[whole()] * 3,
        out_shape=[pltpu.VMEM(part.shape, F32), part, pltpu.VMEM((ZD * channels, cells), BF16)],
        scratch_shapes=[pltpu.VMEM((3 * ZD * channels, cells), BF16)],
        compiler_params=params(),
        name="gradient",
    )(el, em, eh, e_below, e_above, plain)
    arrived = exchanged(send, "slab", 1)
    drho_low, drho_high = pl.pallas_call(
        backward_kernel,
        in_specs=[whole()] * 6,
        out_specs=[whole()] * 2,
        out_shape=[half, half],
        scratch_shapes=scratch,
        compiler_params=params(),
        name="backward",
    )(ed, eu, f_below, f_above, sums, backward)
    drho_below, drho_above = ring(drho_high, "slab", 1), ring(drho_low, "slab", -1)

    total = (keep + arrived.astype(F32)).astype(BF16)
    turns = (lax.axis_size("rep") - 1).bit_length()
    for turn in range(turns):
        arrived = exchanged(total, "rep", 1 << (turns - 1 - turn))
        total = total + arrived
    strides = [1 << i for i in range(1, (lax.axis_size("slab") - 1).bit_length())]
    for stride in strides[:-2]:
        arrived = exchanged(total, "slab", stride)
        total = total + arrived
    near, far = strides[-2:]
    across = [exchanged(total, "slab", s) for s in (near, far, near | far)]
    one, two, three = (value.astype(F32) for value in across)
    total = (total.astype(F32) + one) + (two + three)
    other = exchanged(total, "slab", 1)

    groups = lax.axis_size("rep") * lax.axis_size("slab")
    conv_grad, mix_grad = pl.pallas_call(
        functools.partial(
            finish_kernel,
            conv_scale=math.sqrt(groups * ZD * cells),
            mix_scale=math.sqrt(groups * atoms),
        ),
        in_specs=[whole()] * 4,
        out_specs=[whole()] * 2,
        out_shape=[
            jax.ShapeDtypeStruct(conv_w.shape, F32),
            jax.ShapeDtypeStruct(w_mix.shape, F32),
        ],
        compiler_params=params(),
        name="finish",
    )(total, other, w_mix, conv_w)

    potential, feats_grad = gather(
        (phi_below, phi_low, phi_high, phi_above),
        (drho_below, drho_low, drho_high, drho_above),
        held, atom_ids, cell_ids, live, w_mix, atoms,
    )
    return potential[None], feats_grad[None], conv_grad, mix_grad


def solution(mesh):
    return jax.shard_map(
        local,
        mesh=mesh,
        in_specs=(
            P("rep", None, "slab"),
            P("rep", "slab", None, None),
            P("rep", "slab"),
            P("rep", "slab"),
            P("rep", "slab"),
            P(),
            P(),
            P("rep", None, "slab"),
        ),
        out_specs=(P("rep", None, "slab"), P("rep", None, "slab"), P(), P()),
        check_vma=False,
    )
```

```python
import functools
import math

import jax
import jax.numpy as jnp
from jax import lax
from jax.experimental import pallas as pl
from jax.experimental.pallas import tpu as pltpu
from jax.sharding import PartitionSpec as P

GY = 32
GX = 64
ZD = 4
ZH = 2
F32 = jnp.float32
BF16 = jnp.bfloat16
VMEM_LIMIT = 16 * 1024 * 1024


def params(*semantics):
    return pltpu.CompilerParams(
        dimension_semantics=semantics or None, vmem_limit_bytes=VMEM_LIMIT
    )


def whole():
    return pl.BlockSpec(memory_space=pltpu.VMEM)


def copies(pairs, sems):
    return [
        pltpu.make_async_copy(source, target, sems.at[i])
        for i, (source, target) in enumerate(pairs)
    ]


def add_tiles(tiles, atom_ref, cell_ref, live, source, weight_ref, total):
    for j in range(tiles.start, tiles.stop):
        picked = source[atom_ref[0, j]]
        picked = jnp.where(j < live, picked, jnp.zeros_like(picked))
        total[cell_ref[0, j]] += jnp.dot(
            picked, weight_ref[j], preferred_element_type=F32
        )


def split_atoms(field, source):
    tile_a = source.shape[2]
    for a in range(source.shape[0]):
        source[a] = field[:, a * tile_a : (a + 1) * tile_a]


def write_parts(total, refs):
    first = 0
    for ref in refs:
        count = ref.shape[0]
        ref[...] = total[first : first + count].astype(BF16)
        first += count


def first_deposit_kernel(
    atom_hbm, cell_hbm, live_ref, feats_hbm, weight_hbm,
    down_ref, middle_ref, up_ref, weight_ref,
    atom_ref, cell_ref, small_sems, source, total, feats, weight_sems,
):
    chunks = weight_sems.shape[0]
    per_chunk = weight_ref.shape[0] // chunks
    small = copies(
        ((atom_hbm, atom_ref), (cell_hbm, cell_ref), (feats_hbm, feats)), small_sems
    )
    parts = [slice(i * per_chunk, (i + 1) * per_chunk) for i in range(chunks)]
    large = copies([(weight_hbm.at[p], weight_ref.at[p]) for p in parts], weight_sems)
    ahead = chunks
    for copy in small + large[:ahead]:
        copy.start()
    total[...] = jnp.zeros_like(total)
    for copy in small:
        copy.wait()
    split_atoms(feats[...], source)
    live = live_ref[0, 0]
    for i, (part, copy) in enumerate(zip(parts, large)):
        copy.wait()
        if i + ahead < chunks:
            large[i + ahead].start()
        add_tiles(part, atom_ref, cell_ref, live, source, weight_ref, total)
    write_parts(total, (down_ref, middle_ref, up_ref))


def second_deposit_kernel(
    atom_hbm, cell_hbm, live_ref, cot_ref, weight_ref,
    *rest,
):
    *parts, atom_ref, cell_ref, small_sems, source, total = rest
    small = copies(((atom_hbm, atom_ref), (cell_hbm, cell_ref)), small_sems)
    for copy in small:
        copy.start()
    total[...] = jnp.zeros_like(total)
    split_atoms(cot_ref[...], source)
    for copy in small:
        copy.wait()
    tiles = slice(0, weight_ref.shape[0])
    add_tiles(tiles, atom_ref, cell_ref, live_ref[0, 0], source, weight_ref, total)
    write_parts(total, parts)


def in_hbm(*values):
    return [pltpu.with_memory_space_constraint(value, pltpu.HBM) for value in values]


def hbm():
    return pl.BlockSpec(memory_space=pltpu.HBM)


def list_scratch(atom_ids, cell_ids):
    return [
        pltpu.SMEM(atom_ids.shape, jnp.int32),
        pltpu.SMEM(cell_ids.shape, jnp.int32),
        pltpu.SemaphoreType.DMA((3,)),
    ]


def list_specs():
    return [hbm(), hbm(), pl.BlockSpec(memory_space=pltpu.SMEM)]


def deposit_shapes(field, weights, planes_of):
    channels, atoms = field.shape
    _, tile_a, tile_c = weights.shape
    quarters = GY * GX // tile_c
    parts = [
        pltpu.VMEM((planes * quarters, channels, tile_c), BF16)
        for planes in planes_of
    ]
    scratch = [
        pltpu.VMEM((atoms // tile_a, channels, tile_a), BF16),
        pltpu.VMEM(((ZD + 2 * ZH) * quarters, channels, tile_c), F32),
    ]
    return parts, scratch


def first_deposit(feats, weights, atom_ids, cell_ids, live):
    parts, scratch = deposit_shapes(feats, weights, (ZH + 1, ZD - 2, ZH + 1))
    return pl.pallas_call(
        first_deposit_kernel,
        in_specs=list_specs() + [hbm()] * 2,
        out_specs=[whole()] * 4,
        out_shape=parts + [pltpu.VMEM(weights.shape, BF16)],
        scratch_shapes=list_scratch(atom_ids, cell_ids)
        + scratch
        + [pltpu.VMEM(feats.shape, BF16), pltpu.SemaphoreType.DMA((2,))],
        compiler_params=params(),
        name="first_deposit",
    )(*in_hbm(atom_ids, cell_ids), live, *in_hbm(feats, weights))


def second_deposit(cot, weights, atom_ids, cell_ids, live):
    parts, scratch = deposit_shapes(cot, weights, (ZH, 1, ZD - 2, 1, ZH))
    return pl.pallas_call(
        second_deposit_kernel,
        in_specs=list_specs() + [whole()] * 2,
        out_specs=[whole()] * len(parts),
        out_shape=parts,
        scratch_shapes=list_scratch(atom_ids, cell_ids) + scratch,
        compiler_params=params(),
        name="second_deposit",
    )(*in_hbm(atom_ids, cell_ids), live, cot, weights)


def toeplitz_kernel(conv_ref, forward_ref, backward_ref):
    channels = conv_ref.shape[1]
    for flip, out_ref in ((False, forward_ref), (True, backward_ref)):
        for dy in range(3):
            bands = []
            for dx in range(3):
                parts = []
                for dz in range(3):
                    if flip:
                        k = 9 * (2 - dz) + 3 * (2 - dy) + (2 - dx)
                        parts.append(conv_ref[k].astype(F32).T)
                    else:
                        parts.append(conv_ref[9 * dz + 3 * dy + dx].astype(F32))
                bands.append(jnp.concatenate(parts, axis=1))
            for po in range(ZD):
                pieces = []
                for band in bands:
                    if po:
                        pieces.append(jnp.zeros((channels, po * channels), F32))
                    pieces.append(band)
                    rest = (ZD - 1 - po) * channels
                    if rest:
                        pieces.append(jnp.zeros((channels, rest), F32))
                row = (dy * ZD + po) * channels
                out_ref[row : row + channels] = jnp.concatenate(pieces, axis=1).astype(
                    BF16
                )


def toeplitz(conv_w):
    channels = conv_w.shape[1]
    shape = pltpu.VMEM((3 * ZD * channels, 3 * (ZD + 2) * channels), BF16)
    return pl.pallas_call(
        toeplitz_kernel,
        in_specs=[whole()],
        out_specs=[whole()] * 2,
        out_shape=[shape, shape],
        compiler_params=params(),
        name="toeplitz",
    )(conv_w)


def joined_planes(own, other, quarters):
    def blocks(pieces):
        return [
            ref[q]
            for ref, first, count in pieces
            for q in range(first * quarters, (first + count) * quarters)
        ]

    sums = [a.astype(F32) + b.astype(F32) for a, b in zip(blocks(own), blocks(other))]
    return [
        jnp.concatenate(sums[i : i + quarters], axis=1)
        for i in range(0, len(sums), quarters)
    ]


def store_shifted(out_ref, row, value):
    rows, cells = value.shape
    group = out_ref.shape[0] // 3
    wide = 2 * GX
    x = lax.rem(lax.broadcasted_iota(jnp.int32, (rows, wide), 1), GX)
    out_ref[group + row : group + row + rows] = value
    for first in range(0, cells, wide):
        cols = slice(first, first + wide)
        part = value[:, cols]
        out_ref[row : row + rows, cols] = jnp.where(
            x == 0, pltpu.roll(part, GX + 1, 1), pltpu.roll(part, 1, 1)
        )
        out_ref[2 * group + row : 2 * group + row + rows, cols] = jnp.where(
            x == GX - 1, pltpu.roll(part, GX - 1, 1), pltpu.roll(part, wide - 1, 1)
        )


def conv_planes(matrix_ref, shifted, partial, low_ref, high_ref):
    cells = shifted.shape[1]
    chunk = low_ref.shape[2]
    width = chunk // 2
    for first in range(0, cells, width):
        cols = slice(first, first + width)
        partial[:, cols] = jnp.dot(
            matrix_ref[...], shifted[:, cols], preferred_element_type=F32
        )
    channels = low_ref.shape[1]
    quarters = cells // chunk
    third = ZD * channels
    wide = 2 * GX
    count = cells // wide
    lane = lax.broadcasted_iota(jnp.int32, (channels, wide), 1)
    for po in range(ZD):

        def group(dy, j):
            row = dy * third + po * channels
            first = (j % count) * wide
            return partial[row : row + channels, first : first + wide]

        out_ref = low_ref if po < ZH else high_ref
        block = (po % ZH) * quarters
        before = group(0, count - 1) + group(2, 0)
        for j in range(count):
            after = group(0, j) + group(2, j + 1)
            mixed = jnp.where(lane < GX, after, before)
            result = (group(1, j) + pltpu.roll(mixed, GX, 1)).astype(BF16)
            first = j * wide % chunk
            out_ref[block + j * wide // chunk, :, first : first + wide] = result
            before = after


def forward_kernel(
    down, middle, up, below, above, mix_ref, matrix_ref,
    low_ref, high_ref, plain_ref, shifted, partial,
):
    channels = mix_ref.shape[0]
    quarters = low_ref.shape[0] // ZH
    own = ((down, 1, ZH), (middle, 0, ZD - 2), (up, 0, ZH))
    other = ((below, 0, ZH + 1), (above, 0, ZH + 1))
    for p, plane in enumerate(joined_planes(own, other, quarters)):
        plane = plane.astype(BF16)
        store_shifted(plain_ref, p * channels, plane)
        mixed = jnp.dot(mix_ref[...], plane, preferred_element_type=F32)
        store_shifted(shifted, p * channels, mixed.astype(BF16))
    conv_planes(matrix_ref, shifted, partial, low_ref, high_ref)


def gradient_kernel(
    low, middle, high, below, above, shifted,
    keep_ref, send_ref, sums_ref, upstream,
):
    channels = low.shape[1]
    quarters = low.shape[0]
    cells = shifted.shape[1]
    own = ((low, 0, 1), (middle, 0, ZD - 2), (high, 0, 1))
    planes = joined_planes(own, ((below, 0, ZH), (above, 0, ZH)), quarters)
    third = ZD * channels
    for p, plane in enumerate(planes):
        row = p * channels
        plane = plane.astype(BF16)
        sums_ref[row : row + channels] = plane
        upstream[row : row + channels] = pltpu.roll(plane, cells - GX, 1)
        upstream[third + row : third + row + channels] = plane
        upstream[2 * third + row : 2 * third + row + channels] = pltpu.roll(plane, GX, 1)
    wide = (ZD + 2) * channels
    blocks = []
    for dx in range(3):
        product = lax.dot_general(
            upstream[...],
            shifted[dx * wide : (dx + 1) * wide],
            (((1,), (1,)), ((), ())),
            preferred_element_type=F32,
        )
        for dy in range(3):
            block = None
            for po in range(ZD):
                row = (dy * ZD + po) * channels
                piece = product[
                    row : row + channels, po * channels : (po + 3) * channels
                ]
                block = piece if block is None else block + piece
            blocks.append(
                jnp.concatenate([block, jnp.zeros((channels, channels), F32)], axis=1)
            )
    half = keep_ref.shape[0]
    grads = jnp.concatenate(blocks, axis=0)
    first, second = grads[:half], grads[half:]
    odd = lax.rem(lax.axis_index("slab"), 2) == 1

    @pl.when(odd)
    def _():
        keep_ref[...] = second.astype(keep_ref.dtype)
        send_ref[...] = first.astype(send_ref.dtype)

    @pl.when(jnp.logical_not(odd))
    def _():
        keep_ref[...] = first.astype(keep_ref.dtype)
        send_ref[...] = second.astype(send_ref.dtype)


def backward_kernel(
    down, up, below, above, sums_ref, matrix_ref, low_ref, high_ref, shifted, partial
):
    channels = low_ref.shape[1]
    quarters = below.shape[0]
    (first,) = joined_planes(((down, 1, 1),), ((below, 0, 1),), quarters)
    (last,) = joined_planes(((up, 0, 1),), ((above, 0, 1),), quarters)
    store_shifted(shifted, 0, first.astype(BF16))
    for p in range(ZD):
        rows = slice(p * channels, (p + 1) * channels)
        store_shifted(shifted, (p + 1) * channels, sums_ref[rows])
    store_shifted(shifted, (ZD + 1) * channels, last.astype(BF16))
    conv_planes(matrix_ref, shifted, partial, low_ref, high_ref)


def gather_kernel(
    atom_ref, cell_ref, live_ref, weight_ref, mix_ref,
    a0, a1, a2, a3, b0, b1, b2, b3, potential_ref, grad_ref, field, total,
):
    channels = mix_ref.shape[0]
    tiles, tile_a, tile_c = weight_ref.shape
    half = tile_c // 2
    first = 0
    for a, b in ((a0, b0), (a1, b1), (a2, b2), (a3, b3)):
        count = a.shape[0]
        for i, cols in enumerate((slice(0, half), slice(half, tile_c))):
            row = 2 * i * channels
            field[first : first + count, row : row + channels] = a[:, :, cols]
            field[first : first + count, row + channels : row + 2 * channels] = b[
                :, :, cols
            ]
        first += count
    total[...] = jnp.zeros_like(total)
    live = live_ref[0, 0]
    lane = lax.broadcasted_iota(jnp.int32, (2 * channels, 2 * tile_a), 1)
    for j in range(0, tiles, 2):
        pair = (j, j + 1)
        left = jnp.concatenate([field[cell_ref[0, t]] for t in pair], axis=0)
        right = jnp.concatenate(
            [
                weight_ref[t, :, cols]
                for t in pair
                for cols in (slice(0, half), slice(half, tile_c))
            ],
            axis=0,
        )
        product = lax.dot_general(
            left, right, (((1,), (1,)), ((), ())), preferred_element_type=F32
        )
        for i, t in enumerate(pair):
            row, col = 4 * i * channels, 2 * i * tile_a
            both = jnp.where(
                lane < tile_a,
                product[row : row + 2 * channels, col : col + 2 * tile_a],
                product[row + 2 * channels : row + 4 * channels, col : col + 2 * tile_a],
            )
            total[atom_ref[0, t]] += jnp.where(t < live, both, jnp.zeros_like(both))

    for a in range(0, total.shape[0], 2):
        lower, upper = total[a], total[a + 1]
        pair = jnp.where(
            lane < tile_a,
            lower + pltpu.roll(lower, tile_a, 1),
            upper + pltpu.roll(upper, tile_a, 1),
        ).astype(BF16)
        cols = slice(a * tile_a, (a + 2) * tile_a)
        potential_ref[:, cols] = pair[:channels]
        grad_ref[:, cols] = lax.dot_general(
            mix_ref[...], pair[channels:], (((0,), (0,)), ((), ())),
            preferred_element_type=F32,
        ).astype(BF16)


def gather(phi, drho, weights, atom_ids, cell_ids, live, w_mix, atoms):
    _, tile_a, tile_c = weights.shape
    channels = w_mix.shape[0]
    blocks = sum(part.shape[0] for part in phi)
    shape = jax.ShapeDtypeStruct((channels, atoms), BF16)
    return pl.pallas_call(
        gather_kernel,
        in_specs=[pl.BlockSpec(memory_space=pltpu.SMEM)] * 3 + [whole()] * 10,
        out_specs=[whole()] * 2,
        out_shape=[shape, shape],
        scratch_shapes=[
            pltpu.VMEM((blocks, 4 * channels, tile_c // 2), BF16),
            pltpu.VMEM((atoms // tile_a, 2 * channels, 2 * tile_a), F32),
        ],
        compiler_params=params(),
        name="gather",
    )(atom_ids, cell_ids, live, weights, w_mix, *phi, *drho)


def finish_kernel(
    mine_ref, other_ref, mix_ref, conv_ref, conv_out, mix_out,
    *, conv_scale, mix_scale,
):
    channels = mix_ref.shape[0]
    mine, other = mine_ref[...].astype(F32), other_ref[...].astype(F32)
    odd = lax.rem(lax.axis_index("slab"), 2) == 1
    total = jnp.concatenate(
        [jnp.where(odd, other, mine), jnp.where(odd, mine, other)], axis=0
    )
    mix = mix_ref[...]
    acc = jnp.zeros((channels, channels), F32)
    for dz in range(3):
        part = total[:, dz * channels : (dz + 1) * channels]
        upper = part.astype(BF16)
        pieces = (upper, (part - upper.astype(F32)).astype(BF16))
        kernels = jnp.concatenate(
            [conv_ref[9 * dz + 3 * (n % 3) + n // 3] for n in range(9)], axis=0
        )
        scaled = jnp.zeros(part.shape, F32)
        for piece in pieces:
            scaled = scaled + lax.dot_general(
                piece, mix, (((1,), (1,)), ((), ())), preferred_element_type=F32
            )
            acc = acc + lax.dot_general(
                kernels, piece, (((0,), (0,)), ((), ())), preferred_element_type=F32
            )
        scaled = scaled * (1.0 / conv_scale)
        for n in range(9):
            conv_out[9 * dz + 3 * (n % 3) + n // 3] = scaled[
                n * channels : (n + 1) * channels
            ]
    mix_out[...] = acc * (1.0 / mix_scale)


def ring(value, axis, steps):
    count = lax.axis_size(axis)
    pairs = [(source, (source + steps) % count) for source in range(count)]
    return pltpu.with_memory_space_constraint(
        lax.ppermute(value, axis, pairs), pltpu.VMEM
    )


def exchanged(value, axis, stride):
    count = lax.axis_size(axis)
    return lax.ppermute(value, axis, [(i, i ^ stride) for i in range(count)])


def local(feats, tile_weight, tile_atom, tile_cell, tile_live, w_mix, conv_w, cotangent):
    return step(
        feats[0], tile_weight[0], tile_atom, tile_cell, tile_live,
        w_mix, conv_w, cotangent[0],
    )


def step(feats, weights, atom_ids, cell_ids, live, w_mix, conv_w, cot):
    channels, atoms = feats.shape
    tile_c = weights.shape[2]
    quarters = GY * GX // tile_c
    cells = GY * GX
    smem = pl.BlockSpec(memory_space=pltpu.SMEM)

    dd, dm, du, held = first_deposit(feats, weights, atom_ids, cell_ids, live)
    d_below, d_above = ring(du, "slab", 1), ring(dd, "slab", -1)
    ed, el, em, eh, eu = second_deposit(cot, held, atom_ids, cell_ids, live)
    e_below, e_above = ring(eu, "slab", 1), ring(ed, "slab", -1)
    f_below, f_above = ring(eh, "slab", 1), ring(el, "slab", -1)
    forward, backward = toeplitz(conv_w)

    half = pltpu.VMEM((ZH * quarters, channels, tile_c), BF16)
    rows = (ZD + 2) * channels
    scratch = [
        pltpu.VMEM((3 * rows, cells), BF16),
        pltpu.VMEM((3 * ZD * channels, cells), F32),
    ]
    phi_low, phi_high, plain = pl.pallas_call(
        forward_kernel,
        in_specs=[whole()] * 7,
        out_specs=[whole()] * 3,
        out_shape=[half, half, pltpu.VMEM((3 * rows, cells), BF16)],
        scratch_shapes=scratch,
        compiler_params=params(),
        name="forward",
    )(dd, dm, du, d_below, d_above, w_mix, forward)
    phi_below, phi_above = ring(phi_high, "slab", 1), ring(phi_low, "slab", -1)

    part = pltpu.VMEM((9 * channels // 2, 4 * channels), BF16)
    keep, send, sums = pl.pallas_call(
        gradient_kernel,
        in_specs=[whole()] * 6,
        out_specs=[whole()] * 3,
        out_shape=[pltpu.VMEM(part.shape, F32), part, pltpu.VMEM((ZD * channels, cells), BF16)],
        scratch_shapes=[pltpu.VMEM((3 * ZD * channels, cells), BF16)],
        compiler_params=params(),
        name="gradient",
    )(el, em, eh, e_below, e_above, plain)
    arrived = exchanged(send, "slab", 1)
    drho_low, drho_high = pl.pallas_call(
        backward_kernel,
        in_specs=[whole()] * 6,
        out_specs=[whole()] * 2,
        out_shape=[half, half],
        scratch_shapes=scratch,
        compiler_params=params(),
        name="backward",
    )(ed, eu, f_below, f_above, sums, backward)
    drho_below, drho_above = ring(drho_high, "slab", 1), ring(drho_low, "slab", -1)

    total = (keep + arrived.astype(F32)).astype(BF16)
    turns = (lax.axis_size("rep") - 1).bit_length()
    for turn in range(turns):
        arrived = exchanged(total, "rep", 1 << (turns - 1 - turn))
        total = total + arrived
    strides = [1 << i for i in range(1, (lax.axis_size("slab") - 1).bit_length())]
    for stride in strides[:-2]:
        arrived = exchanged(total, "slab", stride)
        total = total + arrived
    near, far = strides[-2:]
    across = [exchanged(total, "slab", s) for s in (near, far, near | far)]
    one, two, three = (value.astype(F32) for value in across)
    total = (total.astype(F32) + one) + (two + three)
    other = exchanged(total, "slab", 1)

    groups = lax.axis_size("rep") * lax.axis_size("slab")
    conv_grad, mix_grad = pl.pallas_call(
        functools.partial(
            finish_kernel,
            conv_scale=math.sqrt(groups * ZD * cells),
            mix_scale=math.sqrt(groups * atoms),
        ),
        in_specs=[whole()] * 4,
        out_specs=[whole()] * 2,
        out_shape=[
            jax.ShapeDtypeStruct(conv_w.shape, F32),
            jax.ShapeDtypeStruct(w_mix.shape, F32),
        ],
        compiler_params=params(),
        name="finish",
    )(total, other, w_mix, conv_w)

    potential, feats_grad = gather(
        (phi_below, phi_low, phi_high, phi_above),
        (drho_below, drho_low, drho_high, drho_above),
        held, atom_ids, cell_ids, live, w_mix, atoms,
    )
    return potential[None], feats_grad[None], conv_grad, mix_grad


def solution(mesh):
    return jax.shard_map(
        local,
        mesh=mesh,
        in_specs=(
            P("rep", None, "slab"),
            P("rep", "slab", None, None),
            P("rep", "slab"),
            P("rep", "slab"),
            P("rep", "slab"),
            P(),
            P(),
            P("rep", None, "slab"),
        ),
        out_specs=(P("rep", None, "slab"), P("rep", None, "slab"), P(), P()),
        check_vma=False,
    )
```
